512 devices in a mesh: span: 64 (over x, z_lo, y), col: 8 (over z_hi, core).
Axes of the slice: x: 4, y: 4, z: 16 (z_hi: 4, z_lo: 4; z = z_hi * 4 + z_lo), core: 2. Of those that a mesh axis runs over, the one named last changes fastest.
Arguments:
- adjoint_field: float32 [3, 512, 16, 1024], P(None, 'span', None, 'col'), may hold values from -6 to 6
- base_flow: float32 [3, 512, 16, 1024], P(None, 'span', None, 'col'), may hold values from -5 to 5
- metric_diag: bfloat16 [3, 512, 16, 1024], P(None, 'span', None, 'col'), may hold values from 1 to 2
- metric_cross: bfloat16 [3, 512, 16, 1024], P(None, 'span', None, 'col'), may hold values from -0.44921875 to 0.44921875
- jacobian: float32 [512, 16, 1024], P('span', None, 'col'), may hold values from 0.5 to 2
Outputs:
- advanced: float32 [3, 512, 16, 1024], P(None, 'span', None, 'col')
The draws below stay inside these ranges and needn't reach their ends.
All inputs are finite; a program needn't handle non-finite values.
Results may differ from the reference program's by a relative error of at most 0.0003.
Values sent between devices are 32-bit elements; how exact they have to be, the bound alone decides.
A program may use at most 64 MiB of HBM per device.

```python
import math
import jax
import jax.numpy as jnp
import numpy as np
from jax import lax

NX = 512
NY = 16
NZ = 1024


def steps_of(key, shape, cuts, low, largest):
    factor_of = 1.0
    for dim, parts in cuts:
        draws = jax.random.uniform(jax.random.fold_in(jax.random.fold_in(key, 6), dim), (parts,), jnp.float32, low / len(cuts), largest / len(cuts))
        factor_of = factor_of * jnp.repeat(jnp.exp(draws), shape[dim] // parts).reshape((-1,) + (1,) * (len(shape) - 1 - dim))
    return factor_of


def scatter_about(own_key, dims, width, reach, split=(), kind=jnp.bfloat16):
    values = jax.random.normal(own_key, dims, jnp.float32) * width
    if len(split) > 0:
        values = steps_of(own_key, dims, split, -0.22, 0.18) * values
    return jnp.clip(values, min=-reach, max=reach).astype(kind)


def setup_inputs(seed: int = 0) -> dict:
    splits = jax.random.split(jax.random.key(seed), 6)
    return {
        "adjoint_field": scatter_about(splits[0], (3, NX, NY, NZ), 1.0, 6.0, ((1, 64), (3, 8)), jnp.float32),
        "base_flow": scatter_about(splits[1], (3, NX, NY, NZ), 1.0, 5.0, ((1, 64), (3, 8)), jnp.float32),
        "metric_diag": jnp.clip(1.0 + 1.0 * jax.random.uniform(splits[2], (3, NX, NY, NZ), jnp.float32) ** steps_of(splits[2], (3, NX, NY, NZ), ((1, 64), (3, 8)), -0.2, 0.2), 1.0, 2.0).astype(jnp.bfloat16),
        "metric_cross": jnp.clip(jax.random.uniform(splits[3], (3, NX, NY, NZ), jnp.float32, -0.44921875, 0.44921875) * steps_of(splits[3], (3, NX, NY, NZ), ((1, 64), (3, 8)), -0.4, 0.0), -0.44921875, 0.44921875).astype(jnp.bfloat16),
        "jacobian": jnp.clip(jnp.exp(math.log(2.0) - 1.3862944 * jax.random.uniform(splits[4], (NX, NY, NZ), jnp.float32) ** steps_of(splits[4], (NX, NY, NZ), ((0, 64), (2, 8)), -0.2, 0.2)), 0.5, 2.0),
    }


HIGH = lax.Precision.HIGHEST
VISCOSITY = 0.05
STEP_SIZE = 0.01
GLL_INNER = [-0.8717401485096066, -0.5917001814331423, -0.2092992179024789, 0.2092992179024789, 0.5917001814331423, 0.8717401485096066]
GAUSS_POINTS = [-0.9815606342467192, -0.9041172563704749, -0.7699026741943047, -0.5873179542866175, -0.3678314989981802, -0.1252334085114689, 0.1252334085114689, 0.3678314989981802, 0.5873179542866175, 0.7699026741943047, 0.9041172563704749, 0.9815606342467192]
GAUSS_WEIGHTS = [0.0471753363865118, 0.1069393259953184, 0.1600783285433462, 0.2031674267230659, 0.2334925365383548, 0.2491470458134028, 0.2491470458134028, 0.2334925365383548, 0.2031674267230659, 0.1600783285433462, 0.1069393259953184, 0.0471753363865118]


def legendre_seven(points):
    previous = points * 0.0 + 1.0
    current = points
    for degree in range(1, 7):
        following = ((2.0 * degree + 1.0) * points * current - degree * previous) / (degree + 1.0)
        previous = current
        current = following
    return current


def node_tables():
    gll_nodes = np.array([-1.0] + GLL_INNER + [1.0])
    values = legendre_seven(gll_nodes)
    node_weights = 2.0 / (56.0 * values * values)
    identity = np.eye(8, dtype=bool)
    spacing = gll_nodes[:, None] - gll_nodes[None, :]
    derivative = np.where(identity, 0.0, values[:, None] / (values[None, :] * np.where(identity, 1.0, spacing)))
    corner_terms = np.concatenate([np.array([-14.0]), np.zeros(6), np.array([14.0])])
    derivative = derivative + np.eye(8) * corner_terms[None, :]
    gauss_nodes = np.array(GAUSS_POINTS)
    gauss_weights = np.array(GAUSS_WEIGHTS)
    numerators = gauss_nodes[:, None, None] - gll_nodes[None, None, :]
    denominators = np.where(identity, 1.0, spacing)[None]
    ratios = np.where(identity[None], 1.0, numerators / denominators)
    interpolation = ratios.prod(axis=2)
    slope_interp = interpolation @ derivative
    return derivative, node_weights, interpolation, slope_interp, gauss_weights


def float_tables():
    return tuple(jnp.asarray(member, jnp.float32) for member in node_tables())


def along_first(vector, matrix):
    leading, first_len, second_len, third_len = vector.shape
    columns = matrix.shape[1]
    blocks = vector.reshape(leading, first_len // columns, columns, second_len, third_len)
    result = jnp.einsum("pi,laimz->lapmz", matrix, blocks, precision=HIGH)
    return result.reshape(leading, -1, second_len, third_len)


def along_second(vector, matrix):
    leading, first_len, second_len, third_len = vector.shape
    columns = matrix.shape[1]
    blocks = vector.reshape(leading, first_len, second_len // columns, columns, third_len)
    result = jnp.einsum("pi,lxaiz->lxapz", matrix, blocks, precision=HIGH)
    return result.reshape(leading, first_len, -1, third_len)


def along_third(vector, matrix, group_size):
    leading, first_len, second_len, third_len = vector.shape
    columns = matrix.shape[1]
    kron_table = jnp.kron(jnp.eye(group_size, dtype=jnp.float32), matrix.T)
    blocks = vector.reshape(leading, first_len, second_len, third_len // (group_size * columns), group_size * columns)
    result = jnp.einsum("lxyzk,kq->lxyzq", blocks, kron_table, precision=HIGH)
    return result.reshape(leading, first_len, second_len, -1)


def interpolate(vector, matrix, group_size):
    return along_third(along_second(along_first(vector, matrix), matrix), matrix, group_size)


def weight_grid(weights, extent):
    nodes_per = weights.shape[0]
    first_axis = jnp.tile(weights, extent[0] // nodes_per)
    second_axis = jnp.tile(weights, extent[1] // nodes_per)
    third_axis = jnp.tile(weights, extent[2] // nodes_per)
    return first_axis[:, None, None] * second_axis[None, :, None] * third_axis[None, None, :]


def transposed_operator(vector, velocity_fine, metric_diag, metric_cross, group_size, tables):
    derivative, node_weights, interpolation, slope_interp, gauss_weights = tables
    grad_first = along_first(vector, derivative)
    grad_second = along_second(vector, derivative)
    grad_third = along_third(vector, derivative, group_size)
    scaled = VISCOSITY * weight_grid(node_weights, vector.shape[1:])
    flux_first = scaled * (metric_diag[0] * grad_first + metric_cross[0] * grad_second + metric_cross[1] * grad_third)
    flux_second = scaled * (metric_cross[0] * grad_first + metric_diag[1] * grad_second + metric_cross[2] * grad_third)
    flux_third = scaled * (metric_cross[1] * grad_first + metric_cross[2] * grad_second + metric_diag[2] * grad_third)
    stiffness = along_first(flux_first, derivative.T) + along_second(flux_second, derivative.T) + along_third(flux_third, derivative.T, group_size)
    fine_field = interpolate(vector, interpolation, group_size)
    weighted = fine_field * weight_grid(gauss_weights, fine_field.shape[1:])
    back_first = along_first(along_second(along_third(velocity_fine[0] * weighted, interpolation.T, group_size), interpolation.T), slope_interp.T)
    back_second = along_first(along_second(along_third(velocity_fine[1] * weighted, interpolation.T, group_size), slope_interp.T), interpolation.T)
    back_third = along_first(along_second(along_third(velocity_fine[2] * weighted, slope_interp.T, group_size), interpolation.T), interpolation.T)
    return stiffness + back_first + back_second + back_third


def add_partners(padded, which_axis):
    nodes_along = padded.shape[which_axis] - 2
    middle_part = lax.slice_in_dim(padded, 1, nodes_along + 1, axis=which_axis)
    next_part = lax.slice_in_dim(padded, 2, nodes_along + 2, axis=which_axis)
    before = lax.slice_in_dim(padded, 0, nodes_along, axis=which_axis)
    position = (jnp.arange(nodes_along) % 8).reshape(tuple(nodes_along if dimension == which_axis else 1 for dimension in range(padded.ndim)))
    return middle_part + jnp.where(position == 7, next_part, 0.0) + jnp.where(position == 0, before, 0.0)


def assemble_global(vector):
    section_one = add_partners(jnp.concatenate([vector[:, -1:], vector, vector[:, :1]], axis=1), 1)
    section_two = add_partners(jnp.concatenate([section_one[:, :, -1:], section_one, section_one[:, :, :1]], axis=2), 2)
    padded = jnp.pad(section_two, ((0, 0), (0, 0), (0, 0), (1, 1)))
    return add_partners(padded, 3)


def apply_global(vector, base_flow, metric_diag, metric_cross, tables):
    slab_total = vector.shape[1] // 8

    def one_slab(slab_index):
        offset = slab_index * 8
        pieces = [lax.dynamic_slice_in_dim(member, offset, 8, axis=1) for member in (vector, base_flow, metric_diag, metric_cross)]
        fine_flow = interpolate(pieces[1], tables[2], 1)
        return transposed_operator(pieces[0], fine_flow, pieces[2], pieces[3], 1, tables)

    stacked = lax.map(one_slab, jnp.arange(slab_total, dtype=jnp.int32))
    return jnp.transpose(stacked, (1, 0, 2, 3, 4)).reshape(vector.shape)


def reference(adjoint_field, base_flow, metric_diag, metric_cross, jacobian):
    tables = float_tables()
    first_term = apply_global(adjoint_field, base_flow, metric_diag, metric_cross, tables)
    mass_terms = jacobian * weight_grid(tables[1], jacobian.shape)
    assembled = assemble_global(jnp.concatenate([first_term, mass_terms[None]], axis=0))
    inverse_mass = 1.0 / assembled[3]
    planes = jacobian.shape[2]
    global_plane = jnp.arange(planes)
    interior = ((global_plane > 0) & (global_plane < planes - 1)).astype(jnp.float32)
    half_state = interior * (adjoint_field - (0.5 * STEP_SIZE) * inverse_mass * assembled[:3])
    second_term = assemble_global(apply_global(half_state, base_flow, metric_diag, metric_cross, tables))
    return interior * (adjoint_field - STEP_SIZE * inverse_mass * second_term)
```

```python
import functools

import jax
import jax.numpy as jnp
import ml_dtypes
import numpy as np
from jax import lax
from jax.experimental import pallas as pl
from jax.experimental.pallas import tpu as pltpu
from jax.sharding import PartitionSpec as P

VISCOSITY = 0.05
STEP_SIZE = 0.01
GLL_INNER = [
    -0.8717401485096066,
    -0.5917001814331423,
    -0.2092992179024789,
    0.2092992179024789,
    0.5917001814331423,
    0.8717401485096066,
]
GAUSS_POINTS = [
    -0.9815606342467192,
    -0.9041172563704749,
    -0.7699026741943047,
    -0.5873179542866175,
    -0.3678314989981802,
    -0.1252334085114689,
    0.1252334085114689,
    0.3678314989981802,
    0.5873179542866175,
    0.7699026741943047,
    0.9041172563704749,
    0.9815606342467192,
]
GAUSS_WEIGHTS = [
    0.0471753363865118,
    0.1069393259953184,
    0.1600783285433462,
    0.2031674267230659,
    0.2334925365383548,
    0.2491470458134028,
    0.2491470458134028,
    0.2334925365383548,
    0.2031674267230659,
    0.1600783285433462,
    0.1069393259953184,
    0.0471753363865118,
]
MESH = pl.DeviceIdType.MESH
F32 = jnp.float32
BF16 = jnp.bfloat16


def legendre_seven(points):
    previous = points * 0.0 + 1.0
    current = points
    for degree in range(1, 7):
        following = ((2.0 * degree + 1.0) * points * current - degree * previous) / (degree + 1.0)
        previous = current
        current = following
    return current


def node_tables():
    gll_nodes = np.array([-1.0] + GLL_INNER + [1.0])
    values = legendre_seven(gll_nodes)
    node_weights = 2.0 / (56.0 * values * values)
    identity = np.eye(8, dtype=bool)
    spacing = gll_nodes[:, None] - gll_nodes[None, :]
    derivative = np.where(
        identity, 0.0, values[:, None] / (values[None, :] * np.where(identity, 1.0, spacing))
    )
    corner_terms = np.concatenate([np.array([-14.0]), np.zeros(6), np.array([14.0])])
    derivative = derivative + np.eye(8) * corner_terms[None, :]
    gauss_nodes = np.array(GAUSS_POINTS)
    gauss_weights = np.array(GAUSS_WEIGHTS)
    numerators = gauss_nodes[:, None, None] - gll_nodes[None, None, :]
    denominators = np.where(identity, 1.0, spacing)[None]
    ratios = np.where(identity[None], 1.0, numerators / denominators)
    interpolation = ratios.prod(axis=2)
    slope_interp = interpolation @ derivative
    return tuple(
        np.asarray(member, np.float32).astype(np.float64)
        for member in (derivative, node_weights, interpolation, slope_interp, gauss_weights)
    )


def halves(matrix):
    high = matrix.astype(np.float32).astype(ml_dtypes.bfloat16)
    low = (matrix - high.astype(np.float64)).astype(np.float32).astype(ml_dtypes.bfloat16)
    return high, low


def left_table(matrix):
    high, low = halves(matrix)
    return np.concatenate([high, high, low], axis=1)


def right_table(matrix):
    high, low = halves(matrix)
    return np.concatenate([high, high, low], axis=0)


def pad_to(matrix, rows, columns):
    return np.pad(matrix, ((0, rows - matrix.shape[0]), (0, columns - matrix.shape[1])))


def operator_tables():
    dm, rho, jm, dj, sigma = node_tables()
    eye8, eye16 = np.eye(8), np.eye(16)
    forward_z = np.concatenate(
        [np.kron(eye16, dm.T), pad_to(np.kron(eye16, jm.T), 128, 256)], axis=1
    )
    back_z = np.concatenate(
        [
            pad_to(np.kron(eye16, jm), 256, 128),
            pad_to(np.kron(eye16, dj), 256, 128),
            np.kron(eye16, dm),
        ],
        axis=0,
    )
    grad_xy = np.concatenate([np.kron(dm, eye8), np.kron(eye8, dm)], axis=0)
    interp_xy = np.kron(jm, jm)
    back_12 = np.concatenate([np.kron(dj.T, jm.T), np.kron(jm.T, dj.T)], axis=1)
    back_3 = np.kron(jm.T, jm.T)
    back_grad = np.concatenate([np.kron(dm.T, eye8), np.kron(eye8, dm.T)], axis=1)
    fine_z = pad_to(np.tile(sigma, 16)[None], 1, 256)
    fine_weights = (np.kron(sigma, sigma)[:, None] * fine_z).astype(np.float32)
    node_weights = (np.kron(rho, rho)[:, None] * np.tile(rho, 16)[None, :]).astype(np.float32)
    return (
        right_table(forward_z),
        left_table(grad_xy),
        left_table(interp_xy),
        left_table(back_12),
        left_table(back_3),
        left_table(back_grad),
        right_table(back_z),
        fine_weights,
        node_weights,
    )


def split(value):
    high = value.astype(BF16)
    low = (value - high.astype(F32)).astype(BF16)
    return high, low


def mm(a, b):
    return jnp.dot(a, b, preferred_element_type=F32)


def stack_rows(value):
    high, low = split(value)
    return jnp.concatenate([high, low, high], axis=0)


def stack_lanes(value):
    high, low = split(value)
    return jnp.concatenate([high, low, high], axis=1)


def kernel(n_span, n_col, *refs):
    (adj_h, base_h, md_h, mc_h, jac_h) = refs[:5]
    consts_h = refs[5:14]
    out_h = refs[14]
    (v_s, b_s, j_s, md_s, mc_s) = refs[15:20]
    consts = refs[20:29]
    (wzf, gxy_t, jxy_t, c12_t, c3_t, dxyb_t, wzb, o3, w3) = consts
    (uw_s, gw_s, o_s, xs0, xr0, xs1, xr1, zs, zr) = refs[29:38]
    (load_sem, out_sem, send_sem, recv_sem) = refs[38:]

    span = lax.axis_index("span")
    col = lax.axis_index("col")
    right, left = lax.rem(span + 1, n_span), lax.rem(span + n_span - 1, n_span)
    up, down = lax.rem(col + 1, n_col), lax.rem(col + n_col - 1, n_col)
    x_peers = ((right, col), (left, col))
    z_peers = (
        (span, up),
        (span, down),
        (right, up),
        (right, down),
        (left, up),
        (left, down),
    )

    loads = []
    for e in range(2):
        half = pl.ds(8 * e, 8)
        loads.append((base_h.at[:, :, half, :], b_s.at[:, e]))
        loads.append((adj_h.at[:, :, half, :], v_s.at[:, e]))
        loads.append((jac_h.at[:, half, :], j_s.at[e]))
    loads.append((md_h, md_s))
    loads.append((mc_h, mc_s))
    loads.extend(zip(consts_h, consts))
    copies = [
        pltpu.make_async_copy(source, target, load_sem.at[i])
        for i, (source, target) in enumerate(loads)
    ]
    for copy in copies:
        copy.start()
    barrier = pltpu.get_barrier_semaphore()
    for peer in x_peers + z_peers:
        pl.semaphore_signal(barrier, inc=1, device_id=peer, device_id_type=MESH)
    for copy in copies:
        copy.wait()

    for d in range(3):
        lines = mm(stack_lanes(b_s[d].reshape(128, 128)), wzf[:, 128:])
        for e in range(2):
            fine = mm(jxy_t[...], stack_rows(lines[64 * e : 64 * e + 64]))
            uw_s[d, e] = fine * o3[...]

    for i in range(3):
        for name, slot in ((md_s, i), (mc_s, 3 + i)):
            plane = name[i].astype(F32)
            for e in range(2):
                part = plane[:, 8 * e : 8 * e + 8, :].reshape(64, 128)
                gw_s[slot, e] = part * (VISCOSITY * w3[...])

    def pair(i, j):
        return i if i == j else 2 + i + j

    def apply_operator(field):
        high, low = split(field)
        lanes = [slice(128 * c, 128 * c + 128) for c in range(3)]
        stacked = jnp.concatenate(
            [jnp.concatenate([high[:, k], low[:, k], high[:, k]], axis=1) for k in lanes], axis=0
        )
        forward = mm(stacked, wzf[...])
        outputs = []
        for e in range(2):
            rows = slice(64 * e, 64 * e + 64)
            planes = jnp.concatenate([high[rows], low[rows], high[rows]], axis=0)
            grads = mm(gxy_t[...], planes)
            flux = [[None] * 3 for _ in range(3)]
            for c in range(3):
                g = (
                    grads[:64, lanes[c]],
                    grads[64:, lanes[c]],
                    forward[128 * c + 64 * e : 128 * c + 64 * e + 64, :128],
                )
                for d in range(3):
                    flux[d][c] = (
                        gw_s[pair(d, 0), e] * g[0]
                        + gw_s[pair(d, 1), e] * g[1]
                        + gw_s[pair(d, 2), e] * g[2]
                    )
            planar = jnp.concatenate(
                [jnp.concatenate(flux[0], axis=1), jnp.concatenate(flux[1], axis=1)], axis=0
            )
            planar_back = mm(dxyb_t[...], stack_rows(planar))
            for c in range(3):
                lines = forward[128 * c + 64 * e : 128 * c + 64 * e + 64, 128:]
                fine = mm(jxy_t[...], stack_rows(lines))
                first = jnp.concatenate([uw_s[0, e] * fine, uw_s[1, e] * fine], axis=0)
                back_12 = mm(c12_t[...], stack_rows(first))
                back_3 = mm(c3_t[...], stack_rows(uw_s[2, e] * fine))
                gathered = jnp.concatenate([back_12, back_3, flux[2][c]], axis=1)
                normal = mm(stack_lanes(gathered), wzb[...])
                outputs.append(normal + planar_back[:, lanes[c]])
        return jnp.concatenate(
            [
                jnp.concatenate(outputs[:3], axis=1),
                jnp.concatenate(outputs[3:], axis=1),
            ],
            axis=0,
        )

    def local_sum(value):
        width = value.shape[1]
        first = value[:64].reshape(8, 8, width)
        second = value[64:].reshape(8, 8, width)
        place = lax.broadcasted_iota(jnp.int32, (8, 8, width), 1)

        def plus(own, other):
            before = pltpu.roll(other, 1, 1)
            after = pltpu.roll(other, 7, 1)
            return own + jnp.where(place == 7, after, jnp.where(place == 0, before, 0.0))

        total = jnp.concatenate(
            [
                plus(first, second).reshape(64, width),
                plus(second, first).reshape(64, width),
            ],
            axis=0,
        )
        lane = lax.broadcasted_iota(jnp.int32, (128, 128), 1)
        low = (lane % 8 == 0) & (lane > 0)
        high = (lane % 8 == 7) & (lane < 127)
        pieces = []
        for c in range(width // 128):
            piece = total[:, 128 * c : 128 * c + 128]
            pieces.append(
                piece
                + jnp.where(
                    high, pltpu.roll(piece, 127, 1), jnp.where(low, pltpu.roll(piece, 1, 1), 0.0)
                )
            )
        return jnp.concatenate(pieces, axis=1)

    row = lax.broadcasted_iota(jnp.int32, (8, 512), 0)
    lane = lax.broadcasted_iota(jnp.int32, (8, 512), 1)
    ends = ((row < 4) & (lane == 128 * row)) | ((row >= 4) & (lane == 128 * (row - 4) + 127))
    ends = ends.astype(F32).astype(BF16)

    def exchange(phase, value, xs, xr):
        width = value.shape[1]
        picks = ends[:, :width]
        high, low = split(value)
        for e in range(2):
            xs[0, 8 * e : 8 * e + 8] = value[64 * e + 56 : 64 * e + 64]
            xs[1, 8 * e : 8 * e + 8] = value[64 * e : 64 * e + 8]
        contract = (((1,), (1,)), ((), ()))
        zs[phase] = lax.dot_general(
            picks, high, contract, preferred_element_type=F32
        ) + lax.dot_general(picks, low, contract, preferred_element_type=F32)
        sends = []
        for i, peer in enumerate(x_peers):
            sends.append(
                pltpu.make_async_remote_copy(
                    src_ref=xs.at[i],
                    dst_ref=xr.at[i],
                    send_sem=send_sem.at[phase, i],
                    recv_sem=recv_sem.at[phase, i],
                    device_id=peer,
                    device_id_type=MESH,
                )
            )
        for i, peer in enumerate(z_peers):
            sends.append(
                pltpu.make_async_remote_copy(
                    src_ref=zs.at[phase],
                    dst_ref=zr.at[phase, i],
                    send_sem=send_sem.at[phase, 2 + i],
                    recv_sem=recv_sem.at[phase, 2 + i],
                    device_id=peer,
                    device_id_type=MESH,
                )
            )
        for copy in sends:
            copy.start()
        return sends

    def gather(phase, value, xr, sends):
        width = value.shape[1]
        for copy in sends:
            copy.wait()
        pieces = []
        for e in range(2):
            pieces.append(value[64 * e : 64 * e + 8] + xr[0, 8 * e : 8 * e + 8])
            pieces.append(value[64 * e + 8 : 64 * e + 56])
            pieces.append(value[64 * e + 56 : 64 * e + 64] + xr[1, 8 * e : 8 * e + 8])
        total = jnp.concatenate(pieces, axis=0)
        side = lax.broadcasted_iota(jnp.int32, (8, 128), 0)
        place = lax.broadcasted_iota(jnp.int32, (8, 128), 1) % 64
        from_down = (side >= 4) & (col > 0)
        from_up = (side < 4) & (col < n_col - 1)

        def choose(below, above):
            return jnp.where(
                from_down, zr[phase, below], jnp.where(from_up, zr[phase, above], 0.0)
            )

        lines = choose(0, 1)
        lines = lines + jnp.where(place < 8, pltpu.roll(choose(2, 3), 72, 1), 0.0)
        lines = lines + jnp.where(place >= 56, pltpu.roll(choose(4, 5), 56, 1), 0.0)
        lines = pltpu.roll(lines, 4, 0)
        columns = jnp.transpose(jnp.concatenate([lines] * 16, axis=0))[:, :8]
        high, low = split(columns)
        picks = ends[:, :width]
        return total + (mm(high, picks) + mm(low, picks))

    lane = lax.broadcasted_iota(jnp.int32, (1, 128), 1)
    wall = ((lane == 0) & (col == 0)) | ((lane == 127) & (col == n_col - 1))
    interior = jnp.where(wall, 0.0, 1.0).astype(F32)

    def field_at(c):
        return v_s[c].reshape(128, 128)

    start = jnp.concatenate([field_at(c) for c in range(3)], axis=1)
    mass = jnp.concatenate([j_s[e].reshape(64, 128) * w3[...] for e in range(2)], axis=0)
    first = local_sum(jnp.concatenate([apply_operator(start), mass], axis=1))
    pl.semaphore_wait(barrier, 8)
    sends = exchange(0, first, xs0, xr0)
    total = gather(0, first, xr0, sends)
    inverse = 1.0 / total[:, 384:]
    half = jnp.concatenate(
        [
            interior
            * (
                start[:, 128 * c : 128 * c + 128]
                - (0.5 * STEP_SIZE) * inverse * total[:, 128 * c : 128 * c + 128]
            )
            for c in range(3)
        ],
        axis=1,
    )
    second = local_sum(apply_operator(half))
    sends = exchange(1, second, xs1, xr1)
    total = gather(1, second, xr1, sends)
    for c in range(3):
        result = interior * (
            field_at(c) - STEP_SIZE * inverse * total[:, 128 * c : 128 * c + 128]
        )
        o_s[c] = result.reshape(2, 8, 8, 128)
    stores = [
        pltpu.make_async_copy(o_s.at[:, e], out_h.at[:, :, pl.ds(8 * e, 8), :], out_sem.at[e])
        for e in range(2)
    ]
    for copy in stores:
        copy.start()
    for copy in stores:
        copy.wait()


def local(n_span, n_col, adjoint_field, base_flow, metric_diag, metric_cross, jacobian):
    consts = operator_tables()
    const_scratch = [pltpu.VMEM(member.shape, jnp.dtype(member.dtype)) for member in consts]
    return pl.pallas_call(
        functools.partial(kernel, n_span, n_col),
        out_shape=jax.ShapeDtypeStruct(adjoint_field.shape, F32),
        in_specs=[pl.BlockSpec(memory_space=pl.ANY)] * 14,
        out_specs=pl.BlockSpec(memory_space=pl.ANY),
        scratch_shapes=[
            pltpu.VMEM((3, 2, 8, 8, 128), F32),
            pltpu.VMEM((3, 2, 8, 8, 128), F32),
            pltpu.VMEM((2, 8, 8, 128), F32),
            pltpu.VMEM((3, 8, 16, 128), BF16),
            pltpu.VMEM((3, 8, 16, 128), BF16),
            *const_scratch,
            pltpu.VMEM((3, 2, 144, 256), F32),
            pltpu.VMEM((6, 2, 64, 128), F32),
            pltpu.VMEM((3, 2, 8, 8, 128), F32),
            pltpu.VMEM((2, 16, 512), F32),
            pltpu.VMEM((2, 16, 512), F32),
            pltpu.VMEM((2, 16, 384), F32),
            pltpu.VMEM((2, 16, 384), F32),
            pltpu.VMEM((2, 8, 128), F32),
            pltpu.VMEM((2, 6, 8, 128), F32),
            pltpu.SemaphoreType.DMA((17,)),
            pltpu.SemaphoreType.DMA((2,)),
            pltpu.SemaphoreType.DMA((2, 8)),
            pltpu.SemaphoreType.DMA((2, 8)),
        ],
        compiler_params=pltpu.CompilerParams(collective_id=0, has_side_effects=True),
    )(
        adjoint_field,
        base_flow,
        metric_diag,
        metric_cross,
        jacobian,
        *[jnp.asarray(member) for member in consts],
    )


def solution(mesh):
    in_specs = (
        P(None, "span", None, "col"),
        P(None, "span", None, "col"),
        P(None, "span", None, "col"),
        P(None, "span", None, "col"),
        P("span", None, "col"),
    )
    out_specs = P(None, "span", None, "col")
    body = functools.partial(local, mesh.shape["span"], mesh.shape["col"])
    return jax.shard_map(body, mesh=mesh, in_specs=in_specs, out_specs=out_specs, check_vma=False)
```

```python
import functools

import jax
import jax.numpy as jnp
import ml_dtypes
import numpy as np
from jax import lax
from jax.experimental import pallas as pl
from jax.experimental.pallas import tpu as pltpu
from jax.sharding import PartitionSpec as P

VISCOSITY = 0.05
STEP_SIZE = 0.01
GLL_INNER = [
    -0.8717401485096066,
    -0.5917001814331423,
    -0.2092992179024789,
    0.2092992179024789,
    0.5917001814331423,
    0.8717401485096066,
]
GAUSS_POINTS = [
    -0.9815606342467192,
    -0.9041172563704749,
    -0.7699026741943047,
    -0.5873179542866175,
    -0.3678314989981802,
    -0.1252334085114689,
    0.1252334085114689,
    0.3678314989981802,
    0.5873179542866175,
    0.7699026741943047,
    0.9041172563704749,
    0.9815606342467192,
]
GAUSS_WEIGHTS = [
    0.0471753363865118,
    0.1069393259953184,
    0.1600783285433462,
    0.2031674267230659,
    0.2334925365383548,
    0.2491470458134028,
    0.2491470458134028,
    0.2334925365383548,
    0.2031674267230659,
    0.1600783285433462,
    0.1069393259953184,
    0.0471753363865118,
]
MESH = pl.DeviceIdType.MESH
F32 = jnp.float32
BF16 = jnp.bfloat16


def legendre_seven(points):
    previous = points * 0.0 + 1.0
    current = points
    for degree in range(1, 7):
        following = ((2.0 * degree + 1.0) * points * current - degree * previous) / (degree + 1.0)
        previous = current
        current = following
    return current


def node_tables():
    gll_nodes = np.array([-1.0] + GLL_INNER + [1.0])
    values = legendre_seven(gll_nodes)
    node_weights = 2.0 / (56.0 * values * values)
    identity = np.eye(8, dtype=bool)
    spacing = gll_nodes[:, None] - gll_nodes[None, :]
    derivative = np.where(
        identity, 0.0, values[:, None] / (values[None, :] * np.where(identity, 1.0, spacing))
    )
    corner_terms = np.concatenate([np.array([-14.0]), np.zeros(6), np.array([14.0])])
    derivative = derivative + np.eye(8) * corner_terms[None, :]
    gauss_nodes = np.array(GAUSS_POINTS)
    gauss_weights = np.array(GAUSS_WEIGHTS)
    numerators = gauss_nodes[:, None, None] - gll_nodes[None, None, :]
    denominators = np.where(identity, 1.0, spacing)[None]
    ratios = np.where(identity[None], 1.0, numerators / denominators)
    interpolation = ratios.prod(axis=2)
    slope_interp = interpolation @ derivative
    return tuple(
        np.asarray(member, np.float32).astype(np.float64)
        for member in (derivative, node_weights, interpolation, slope_interp, gauss_weights)
    )


def halves(matrix):
    high = matrix.astype(np.float32).astype(ml_dtypes.bfloat16)
    low = (matrix - high.astype(np.float64)).astype(np.float32).astype(ml_dtypes.bfloat16)
    return high, low


def left_table(matrix):
    return np.concatenate([halves(matrix)[i] for i in (0, 0, 1)], axis=1)


def right_table(matrix):
    return np.stack(halves(matrix))


def operator_tables():
    dm, rho, jm, dj, sigma = node_tables()
    eye8, eye16 = np.eye(8), np.eye(16)
    ends_lanes = [(c, 15 * s, (2 * c + s) * 12) for c in range(3) for s in range(2)]
    middle_lanes = [(0, a, (a - 1) * 12) for a in range(1, 15)]
    middle_lanes += [(1, a, (13 + a) * 12) for a in range(1, 8)]

    def lines(matrix, lanes, components, width):
        table = np.zeros((components * 128, width))
        for c, a, lane in lanes:
            table[128 * c + 8 * a : 128 * c + 8 * a + 8, lane : lane + 12] = matrix.T
        return table

    flow = np.zeros((128, 640))
    weights_z = np.zeros((1, 640))
    for tile, lanes in enumerate((ends_lanes, middle_lanes, middle_lanes)):
        for c, a, lane in lanes:
            start = lane + (0, 128, 384)[tile]
            element = a + 7 if tile == 2 and c == 1 else a
            flow[8 * element : 8 * element + 8, start : start + 12] = jm.T
            weights_z[0, start : start + 12] = sigma
    weights_xy = np.broadcast_to(np.kron(sigma, sigma)[:, None], (144, 128)).astype(np.float32)
    weights_z = np.broadcast_to(weights_z, (8, 640)).astype(np.float32)
    node_weights = (np.kron(rho, rho)[:, None] * np.tile(rho, 16)[None, :]).astype(np.float32)
    back_ends = np.concatenate(
        [lines(jm, ends_lanes, 3, 128).T, lines(dj, ends_lanes, 3, 128).T], axis=0
    )
    back_middle = np.concatenate(
        [lines(jm, middle_lanes, 2, 256).T, lines(dj, middle_lanes, 2, 256).T], axis=0
    )
    return (
        right_table(np.kron(eye16, dm.T)),
        right_table(np.kron(eye16, dm)),
        left_table(np.concatenate([np.kron(dm, eye8), np.kron(eye8, dm)], axis=0)),
        left_table(np.concatenate([np.kron(dm.T, eye8), np.kron(eye8, dm.T)], axis=1)),
        right_table(flow),
        right_table(lines(jm, ends_lanes, 3, 128)),
        right_table(lines(jm, middle_lanes, 2, 256)),
        left_table(np.kron(jm, jm)),
        left_table(np.concatenate([np.kron(dj.T, jm.T), np.kron(jm.T, dj.T)], axis=1)),
        left_table(np.kron(jm.T, jm.T)),
        right_table(back_ends),
        right_table(back_middle),
        weights_xy,
        weights_z,
        node_weights,
    )


def split(value):
    high = value.astype(BF16)
    low = (value - high.astype(F32)).astype(BF16)
    return high, low


def mm(a, b):
    return jnp.dot(a, b, preferred_element_type=F32)


def mm_right(stacked, table):
    return mm(stacked, jnp.concatenate([table[0], table[0], table[1]], axis=0))


def stack_rows(value):
    high, low = split(value)
    return jnp.concatenate([high, low, high], axis=0)


def stack_lanes(value):
    high, low = split(value)
    return jnp.concatenate([high, low, high], axis=1)


def kernel(n_span, n_col, *refs):
    (adj_h, base_h, md_h, mc_h, jac_h) = refs[:5]
    consts_h = refs[5:20]
    out = refs[20]
    (v_s, b_s, j_s, md_s, mc_s) = refs[21:26]
    consts = refs[26:41]
    (wg, wgb, gxy, gxyb, wflow, wfe, wfm, jxy, c12, c3, wbe, wbm, o_xy, o_z, w3) = consts
    (uw_s, gw_s, xs0, xr0, xs1, xr1, zs, zr, rs, rr) = refs[41:51]
    (load_sem, send_sem, recv_sem) = refs[51:]

    span = lax.axis_index("span")
    col = lax.axis_index("col")
    right, left = lax.rem(span + 1, n_span), lax.rem(span + n_span - 1, n_span)
    up, down = lax.rem(col + 1, n_col), lax.rem(col + n_col - 1, n_col)
    x_peers = ((right, col), (left, col))
    z_peers = ((span, up), (span, down))

    tables = list(zip(consts_h, consts))
    y_halves = [pl.ds(0, 8), pl.ds(8, 8)]
    groups = [
        [(base_h.at[:, :, y_halves[e], :], b_s.at[:, e]) for e in range(2)]
        + [tables[i] for i in (4, 7, 12, 13)],
        [(md_h, md_s), (mc_h, mc_s), tables[14]]
        + [(adj_h.at[:, :, y_halves[e], :], v_s.at[:, e]) for e in range(2)]
        + [(jac_h.at[:, y_halves[e], :], j_s.at[e]) for e in range(2)]
        + tables[:4],
        [tables[i] for i in (5, 8, 9, 10)],
        [tables[i] for i in (6, 11)],
    ]
    loads, used = [], 0
    for group in groups:
        loads.append(
            [
                pltpu.make_async_copy(source, target, load_sem.at[used + i])
                for i, (source, target) in enumerate(group)
            ]
        )
        used += len(group)
    for group in loads:
        for copy in group:
            copy.start()

    def arrive(group):
        for copy in loads[group]:
            copy.wait()

    barrier = pltpu.get_barrier_semaphore()
    for peer in x_peers + z_peers:
        pl.semaphore_signal(barrier, inc=1, device_id=peer, device_id_type=MESH)
    arrive(0)
    planes = []
    for e in range(2):
        rows = jnp.concatenate([b_s[d, e].reshape(64, 128) for d in range(3)], axis=1)
        fine = mm(jxy[...], stack_rows(rows))
        planes.extend(fine[:, 128 * d : 128 * d + 128] for d in range(3))
    fine_weights = o_xy[:, :1] * o_z[:1]
    flow = mm_right(stack_lanes(jnp.concatenate(planes, axis=0)), wflow)
    for e in range(2):
        for d in range(3):
            first = 144 * (3 * e + d)
            uw_s[d, e] = flow[first : first + 144] * fine_weights

    arrive(1)
    for i in range(3):
        for name, slot in ((md_s, i), (mc_s, 3 + i)):
            plane = name[i].astype(F32)
            for e in range(2):
                part = plane[:, 8 * e : 8 * e + 8, :].reshape(64, 128)
                gw_s[slot, e] = part * (VISCOSITY * w3[...])

    lanes = [slice(128 * c, 128 * c + 128) for c in range(4)]
    halves_of = [slice(0, 64), slice(64, 128)]

    def pair(i, j):
        return i if i == j else 2 + i + j

    def stiffness(high, low):
        stacked = jnp.concatenate(
            [jnp.concatenate([high[c], low[c], high[c]], axis=1) for c in range(3)], axis=0
        )
        grad_z = mm_right(stacked, wg)
        planar, fluxes = [], [[None, None] for _ in range(3)]
        for e in range(2):
            wide_high = jnp.concatenate([high[c][halves_of[e]] for c in range(3)], axis=1)
            wide_low = jnp.concatenate([low[c][halves_of[e]] for c in range(3)], axis=1)
            grads = mm(gxy[...], jnp.concatenate([wide_high, wide_low, wide_high], axis=0))
            flux = [[None] * 3 for _ in range(2)]
            for c in range(3):
                start = 128 * c + 64 * e
                g = (
                    grads[:64, lanes[c]],
                    grads[64:, lanes[c]],
                    grad_z[start : start + 64],
                )
                h = [
                    gw_s[pair(d, 0), e] * g[0]
                    + gw_s[pair(d, 1), e] * g[1]
                    + gw_s[pair(d, 2), e] * g[2]
                    for d in range(3)
                ]
                flux[0][c], flux[1][c], fluxes[c][e] = h
            joined = jnp.concatenate([jnp.concatenate(f, axis=1) for f in flux], axis=0)
            planar.append(mm(gxyb[...], stack_rows(joined)))
        normal = mm_right(
            stack_lanes(jnp.concatenate([f for two in fluxes for f in two], axis=0)), wgb
        )
        return jnp.concatenate(planar, axis=0) + jnp.concatenate(
            [normal[128 * c : 128 * c + 128] for c in range(3)], axis=1
        )

    def convection(lines, window):
        pieces = []
        for e in range(2):
            fine = mm(jxy[...], stack_rows(lines[halves_of[e]]))
            planar = jnp.concatenate([uw_s[d, e, :, window] * fine for d in range(2)], axis=0)
            pieces.append(
                (
                    mm(c12[...], stack_rows(planar)),
                    mm(c3[...], stack_rows(uw_s[2, e, :, window] * fine)),
                )
            )
        return pieces

    def end_convection(high, low):
        stacked = jnp.concatenate(high + low + high, axis=1)
        pieces = convection(mm_right(stacked, wfe), slice(0, 128))
        joined = jnp.concatenate([jnp.concatenate(p, axis=1) for p in pieces], axis=0)
        return mm_right(stack_lanes(joined), wbe)

    def middle_convection(field, high, low):
        shifted_high, shifted_low = split(pltpu.roll(field[2], 72, 1))
        stacked = jnp.concatenate(
            [
                jnp.concatenate([high[0], high[2], low[0], low[2], high[0], high[2]], axis=1),
                jnp.concatenate(
                    [high[1], shifted_high, low[1], shifted_low, high[1], shifted_high], axis=1
                ),
            ],
            axis=0,
        )
        both = mm_right(stacked, wfm)
        lines = jnp.concatenate([both[:128], both[128:]], axis=1)
        pieces = convection(lines, slice(128, 640))
        joined = jnp.concatenate(
            [
                jnp.concatenate([part[:, 256 * t : 256 * t + 256] for part in pieces[e]], axis=1)
                for t in range(2)
                for e in range(2)
            ],
            axis=0,
        )
        back = mm_right(stack_lanes(joined), wbm)
        tail = back[:128, 128:] + pltpu.roll(back[128:, 128:], 56, 1)
        return jnp.concatenate([back[:128, :128], back[128:, :128], tail], axis=1)

    def local_sum(value, low, high):
        width, count = value.shape[1], high - low
        two = [value[64 * e + 8 * low : 64 * e + 8 * high] for e in range(2)]
        two = [member.reshape(count, 8, width) for member in two]
        place = lax.broadcasted_iota(jnp.int32, (count, 8, width), 1)
        lane = lax.broadcasted_iota(jnp.int32, (8 * count, 128), 1)
        begins = (lane % 8 == 0) & (lane > 0)
        closes = (lane % 8 == 7) & (lane < 127)
        results = []
        for own, other in ((two[0], two[1]), (two[1], two[0])):
            before = pltpu.roll(other, 1, 1)
            after = pltpu.roll(other, 7, 1)
            total = own + jnp.where(place == 7, after, jnp.where(place == 0, before, 0.0))
            total = total.reshape(8 * count, width)
            pieces = []
            for c in range(width // 128):
                piece = total[:, lanes[c]]
                near = jnp.where(
                    closes,
                    pltpu.roll(piece, 127, 1),
                    jnp.where(begins, pltpu.roll(piece, 1, 1), 0.0),
                )
                pieces.append(piece + near)
            results.append(jnp.concatenate(pieces, axis=1))
        return results

    row = lax.broadcasted_iota(jnp.int32, (8, 512), 0)
    lane = lax.broadcasted_iota(jnp.int32, (8, 512), 1)
    ends = ((row < 4) & (lane == 128 * row)) | ((row >= 4) & (lane == 128 * (row - 4) + 127))
    ends = ends.astype(F32).astype(BF16)
    side = lax.broadcasted_iota(jnp.int32, (8, 128), 0)
    place = lax.broadcasted_iota(jnp.int32, (8, 128), 1) % 64

    def remote(source, target, phase, i, peer):
        return pltpu.make_async_remote_copy(
            src_ref=source,
            dst_ref=target,
            send_sem=send_sem.at[phase, i],
            recv_sem=recv_sem.at[phase, i],
            device_id=peer,
            device_id_type=MESH,
        )

    def send_ends(phase, value):
        width = value.shape[1]
        high, low = split(value)
        contract = (((1,), (1,)), ((), ()))
        tile = lax.dot_general(
            ends[:, :width], high, contract, preferred_element_type=F32
        ) + lax.dot_general(ends[:, :width], low, contract, preferred_element_type=F32)
        after = jnp.where(place % 8 == 7, pltpu.roll(tile, 71, 1), 0.0)
        before = jnp.where(place % 8 == 0, pltpu.roll(tile, 57, 1), 0.0)
        zs[phase] = tile + after + before
        copies = [
            remote(zs.at[phase], zr.at[phase, i], phase, 2 + i, peer)
            for i, peer in enumerate(z_peers)
        ]
        for copy in copies:
            copy.start()
        return copies

    def exchange(phase, value, xs, xr, z_copies):
        faces = [local_sum(value, 7, 8), local_sum(value, 0, 1)]
        for i in range(2):
            for e in range(2):
                xs[i, 8 * e : 8 * e + 8] = faces[i][e]
        x_copies = [
            remote(xs.at[i], xr.at[i], phase, i, peer) for i, peer in enumerate(x_peers)
        ]
        for copy in x_copies:
            copy.start()
        inner = local_sum(value, 1, 7)
        for copy in z_copies:
            copy.wait_recv()
        from_down = (side >= 4) & (col > 0)
        from_up = (side < 4) & (col < n_col - 1)
        lines = jnp.where(from_down, zr[phase, 0], jnp.where(from_up, zr[phase, 1], 0.0))
        rs[phase] = lines
        relays = [
            remote(rs.at[phase], rr.at[phase, i], phase, 4 + i, peer)
            for i, peer in enumerate(x_peers)
        ]
        for copy in relays:
            copy.start()
        for copy in x_copies + relays:
            copy.wait_recv()
        lines = lines + jnp.where(place < 8, pltpu.roll(rr[phase, 0], 72, 1), 0.0)
        lines = lines + jnp.where(place >= 56, pltpu.roll(rr[phase, 1], 56, 1), 0.0)
        lines = pltpu.roll(lines, 4, 0)
        columns = jnp.transpose(jnp.concatenate([lines] * 16, axis=0))[:, :8]
        high, low = split(columns)
        picks = ends[:, : value.shape[1]]
        pieces = []
        for e in range(2):
            pieces.append(faces[1][e] + xr[0, 8 * e : 8 * e + 8])
            pieces.append(inner[e])
            pieces.append(faces[0][e] + xr[1, 8 * e : 8 * e + 8])
        total = jnp.concatenate(pieces, axis=0) + (mm(high, picks) + mm(low, picks))
        for copy in x_copies + z_copies + relays:
            copy.wait_send()
        return total

    lane = lax.broadcasted_iota(jnp.int32, (1, 128), 1)
    wall = ((lane == 0) & (col == 0)) | ((lane == 127) & (col == n_col - 1))
    interior = jnp.where(wall, 0.0, 1.0).astype(F32)

    start = [v_s[c].reshape(128, 128) for c in range(3)]
    mass = jnp.concatenate([j_s[e].reshape(64, 128) * w3[...] for e in range(2)], axis=0)

    pairs = [split(member) for member in start]
    high, low = [p[0] for p in pairs], [p[1] for p in pairs]
    value = stiffness(high, low)
    arrive(2)
    value = jnp.concatenate([value + end_convection(high, low), mass], axis=1)
    pl.semaphore_wait(barrier, 4)
    z_copies = send_ends(0, value)
    arrive(3)
    middle = middle_convection(start, high, low)
    value = jnp.concatenate([value[:, :384] + middle, mass], axis=1)
    total = exchange(0, value, xs0, xr0, z_copies)
    inverse = 1.0 / total[:, lanes[3]]
    half = [
        interior * (start[c] - (0.5 * STEP_SIZE) * inverse * total[:, lanes[c]]) for c in range(3)
    ]

    pairs = [split(member) for member in half]
    high, low = [p[0] for p in pairs], [p[1] for p in pairs]
    value = stiffness(high, low) + end_convection(high, low)
    z_copies = send_ends(1, value)
    value = value + middle_convection(half, high, low)
    total = exchange(1, value, xs1, xr1, z_copies)
    for c in range(3):
        result = interior * (
            v_s[c].reshape(128, 128) - STEP_SIZE * inverse * total[:, lanes[c]]
        )
        for e in range(2):
            out[c, :, 8 * e : 8 * e + 8, :] = result[halves_of[e]].reshape(8, 8, 128)


def local(n_span, n_col, adjoint_field, base_flow, metric_diag, metric_cross, jacobian):
    consts = operator_tables()
    const_scratch = [pltpu.VMEM(member.shape, jnp.dtype(member.dtype)) for member in consts]
    return pl.pallas_call(
        functools.partial(kernel, n_span, n_col),
        out_shape=pltpu.VMEM(adjoint_field.shape, F32),
        in_specs=[pl.BlockSpec(memory_space=pl.ANY)] * 20,
        out_specs=pl.BlockSpec(memory_space=pltpu.VMEM),
        scratch_shapes=[
            pltpu.VMEM((3, 2, 8, 8, 128), F32),
            pltpu.VMEM((3, 2, 8, 8, 128), F32),
            pltpu.VMEM((2, 8, 8, 128), F32),
            pltpu.VMEM((3, 8, 16, 128), BF16),
            pltpu.VMEM((3, 8, 16, 128), BF16),
            *const_scratch,
            pltpu.VMEM((3, 2, 144, 640), F32),
            pltpu.VMEM((6, 2, 64, 128), F32),
            pltpu.VMEM((2, 16, 512), F32),
            pltpu.VMEM((2, 16, 512), F32),
            pltpu.VMEM((2, 16, 384), F32),
            pltpu.VMEM((2, 16, 384), F32),
            pltpu.VMEM((2, 8, 128), F32),
            pltpu.VMEM((2, 2, 8, 128), F32),
            pltpu.VMEM((2, 8, 128), F32),
            pltpu.VMEM((2, 2, 8, 128), F32),
            pltpu.SemaphoreType.DMA((23,)),
            pltpu.SemaphoreType.DMA((2, 6)),
            pltpu.SemaphoreType.DMA((2, 6)),
        ],
        compiler_params=pltpu.CompilerParams(collective_id=0, has_side_effects=True),
    )(
        adjoint_field,
        base_flow,
        metric_diag,
        metric_cross,
        jacobian,
        *[jnp.asarray(member) for member in consts],
    )


def solution(mesh):
    in_specs = (
        P(None, "span", None, "col"),
        P(None, "span", None, "col"),
        P(None, "span", None, "col"),
        P(None, "span", None, "col"),
        P("span", None, "col"),
    )
    out_specs = P(None, "span", None, "col")
    body = functools.partial(local, mesh.shape["span"], mesh.shape["col"])
    return jax.shard_map(body, mesh=mesh, in_specs=in_specs, out_specs=out_specs, check_vma=False)
```

```python
import functools

import jax
import jax.numpy as jnp
import ml_dtypes
import numpy as np
from jax import lax
from jax.experimental import pallas as pl
from jax.experimental.pallas import tpu as pltpu
from jax.sharding import PartitionSpec as P

VISCOSITY = 0.05
STEP_SIZE = 0.01
GLL_INNER = [
    -0.8717401485096066,
    -0.5917001814331423,
    -0.2092992179024789,
    0.2092992179024789,
    0.5917001814331423,
    0.8717401485096066,
]
GAUSS_POINTS = [
    -0.9815606342467192,
    -0.9041172563704749,
    -0.7699026741943047,
    -0.5873179542866175,
    -0.3678314989981802,
    -0.1252334085114689,
    0.1252334085114689,
    0.3678314989981802,
    0.5873179542866175,
    0.7699026741943047,
    0.9041172563704749,
    0.9815606342467192,
]
GAUSS_WEIGHTS = [
    0.0471753363865118,
    0.1069393259953184,
    0.1600783285433462,
    0.2031674267230659,
    0.2334925365383548,
    0.2491470458134028,
    0.2491470458134028,
    0.2334925365383548,
    0.2031674267230659,
    0.1600783285433462,
    0.1069393259953184,
    0.0471753363865118,
]
MESH = pl.DeviceIdType.MESH
F32 = jnp.float32
BF16 = jnp.bfloat16


def legendre_seven(points):
    previous = points * 0.0 + 1.0
    current = points
    for degree in range(1, 7):
        following = ((2.0 * degree + 1.0) * points * current - degree * previous) / (degree + 1.0)
        previous = current
        current = following
    return current


def node_tables():
    gll_nodes = np.array([-1.0] + GLL_INNER + [1.0])
    values = legendre_seven(gll_nodes)
    node_weights = 2.0 / (56.0 * values * values)
    identity = np.eye(8, dtype=bool)
    spacing = gll_nodes[:, None] - gll_nodes[None, :]
    derivative = np.where(
        identity, 0.0, values[:, None] / (values[None, :] * np.where(identity, 1.0, spacing))
    )
    corner_terms = np.concatenate([np.array([-14.0]), np.zeros(6), np.array([14.0])])
    derivative = derivative + np.eye(8) * corner_terms[None, :]
    gauss_nodes = np.array(GAUSS_POINTS)
    gauss_weights = np.array(GAUSS_WEIGHTS)
    numerators = gauss_nodes[:, None, None] - gll_nodes[None, None, :]
    denominators = np.where(identity, 1.0, spacing)[None]
    ratios = np.where(identity[None], 1.0, numerators / denominators)
    interpolation = ratios.prod(axis=2)
    slope_interp = interpolation @ derivative
    return tuple(
        np.asarray(member, np.float32).astype(np.float64)
        for member in (derivative, node_weights, interpolation, slope_interp, gauss_weights)
    )


def halves(matrix):
    high = matrix.astype(np.float32).astype(ml_dtypes.bfloat16)
    low = (matrix - high.astype(np.float64)).astype(np.float32).astype(ml_dtypes.bfloat16)
    return high, low


def left_table(matrix):
    return np.concatenate([halves(matrix)[i] for i in (0, 0, 1)], axis=1)


def right_table(matrix):
    return np.stack(halves(matrix))


def operator_tables():
    dm, rho, jm, dj, sigma = node_tables()
    eye8, eye16 = np.eye(8), np.eye(16)
    ends = [(16 * c + 8 * s, 24 * c + 12 * s) for c in range(3) for s in range(2)]
    middle = [(8 * a, 12 * (a - 1)) for a in range(1, 15)]
    middle += [(128 + 8 * a, 12 * (13 + a)) for a in range(1, 8)]

    def blocks(matrix, places, rows, columns):
        table = np.zeros((rows, columns))
        for first, second in places:
            height, width = matrix.shape
            second = second if width == 12 else first
            table[first : first + height, second : second + width] = matrix
        return table

    to_ends = np.concatenate(
        [blocks(dm.T, ends, 128, 128), blocks(jm.T, ends, 128, 128)], axis=1
    )
    from_ends = np.concatenate(
        [
            blocks(jm.T, ends, 128, 128).T,
            blocks(dj.T, ends, 128, 128).T,
            blocks(dm.T, ends, 128, 128).T,
        ],
        axis=0,
    )
    to_middle = blocks(jm.T, middle, 256, 256)
    from_middle = np.concatenate([to_middle.T, blocks(dj.T, middle, 256, 256).T], axis=0)

    flow_ends, flow_middle = np.zeros((128, 128)), np.zeros((128, 512))
    sigma_z = np.zeros((1, 512))
    for node, gauss in ends:
        element = 0 if node % 16 == 8 else 120
        flow_ends[element : element + 8, gauss : gauss + 12] = jm.T
        sigma_z[0, gauss : gauss + 12] = sigma
    for t in range(2):
        for node, gauss in middle:
            element = node if node < 128 else node - 128 + 56 * t
            flow_middle[element : element + 8, 256 * t + gauss : 256 * t + gauss + 12] = jm.T
    tile = np.zeros(256)
    for node, gauss in middle:
        tile[gauss : gauss + 12] = sigma
    sigma_z[0, 128:256], sigma_z[0, 256:384], sigma_z[0, 384:] = tile[:128], tile[128:], tile[128:]
    flow_middle = np.concatenate([flow_middle[:, :256], flow_middle[:, 384:]], axis=1)
    sigma_z = np.broadcast_to(sigma_z, (8, 512)).astype(np.float32)
    sigma_xy = np.broadcast_to(np.kron(sigma, sigma)[:, None], (144, 128)).astype(np.float32)

    node_weights = (np.kron(rho, rho)[:, None] * np.tile(rho, 16)[None, :]).astype(np.float32)
    choose_ends = np.zeros((128, 128))
    for node, _ in ends:
        element = 0 if node % 16 == 8 else 120
        choose_ends[element : element + 8, node : node + 8] = np.eye(8)
    return {
        "z_grad": right_table(np.kron(eye16, dm.T)),
        "z_grad_back": right_table(np.kron(eye16, dm)),
        "xy_grad": left_table(np.concatenate([np.kron(dm, eye8), np.kron(eye8, dm)], axis=0)),
        "xy_grad_back": left_table(
            np.concatenate([np.kron(dm.T, eye8), np.kron(eye8, dm.T)], axis=1)
        ),
        "xy_interp": left_table(np.kron(jm, jm)),
        "xy_back_12": left_table(
            np.concatenate([np.kron(dj.T, jm.T), np.kron(jm.T, dj.T)], axis=1)
        ),
        "xy_back_3": left_table(np.kron(jm.T, jm.T)),
        "to_ends": right_table(to_ends),
        "from_ends": right_table(from_ends),
        "to_middle": right_table(to_middle),
        "from_middle": right_table(from_middle),
        "flow_ends": right_table(flow_ends),
        "flow_middle": right_table(flow_middle),
        "choose_ends": choose_ends.astype(ml_dtypes.bfloat16),
        "sigma_xy": sigma_xy,
        "sigma_z": sigma_z,
        "node_weights": node_weights,
    }


def split(value):
    high = value.astype(BF16)
    low = (value - high.astype(F32)).astype(BF16)
    return high, low


def mm(a, b):
    return jnp.dot(a, b, preferred_element_type=F32)


def mm_right(stacked, table):
    return mm(stacked, jnp.concatenate([table[0], table[0], table[1]], axis=0))


def stack_rows(value):
    high, low = split(value)
    return jnp.concatenate([high, low, high], axis=0)


def stack_lanes(value):
    high, low = split(value)
    return jnp.concatenate([high, low, high], axis=1)


def kernel(n_span, n_col, names, *refs):
    n_tables = len(names)
    (adj_h, base_h, md_h, mc_h, jac_h) = refs[:5]
    tables_h = dict(zip(names, refs[5 : 5 + n_tables]))
    out = refs[5 + n_tables]
    refs = refs[6 + n_tables :]
    (v_s, b_s, j_s, md_s, mc_s) = refs[:5]
    tables = dict(zip(names, refs[5 : 5 + n_tables]))
    refs = refs[5 + n_tables :]
    (ue_s, um_s, ge_s, gw_s, xs0, xr0, xs1, xr1, zs, zr, rs, rr, dr) = refs[:13]
    (load_sem, send_sem, recv_sem) = refs[13:]

    span = lax.axis_index("span")
    col = lax.axis_index("col")
    right, left = lax.rem(span + 1, n_span), lax.rem(span + n_span - 1, n_span)
    up, down = lax.rem(col + 1, n_col), lax.rem(col + n_col - 1, n_col)
    x_peers = ((right, col), (left, col))
    z_peers = ((span, up), (span, down))
    corner_peers = ((right, up), (right, down), (left, up), (left, down))

    y_halves = [pl.ds(0, 8), pl.ds(8, 8)]
    table = {name: (tables_h[name], tables[name]) for name in names}
    groups = [
        [(base_h.at[:, :, y_halves[e], :], b_s.at[:, e]) for e in range(2)]
        + [table[n] for n in ("xy_interp", "flow_ends", "sigma_xy", "sigma_z")]
        + [(md_h, md_s), (mc_h, mc_s)]
        + [(adj_h.at[:, :, y_halves[e], :], v_s.at[:, e]) for e in range(2)]
        + [table[n] for n in ("choose_ends", "node_weights", "to_ends", "xy_grad")],
        [table[n] for n in ("xy_grad_back", "xy_back_12", "xy_back_3", "from_ends")]
        + [(jac_h.at[:, y_halves[e], :], j_s.at[e]) for e in range(2)],
        [table[n] for n in ("z_grad", "z_grad_back", "flow_middle", "to_middle", "from_middle")],
    ]
    loads, used = [], 0
    for group in groups:
        loads.append(
            [
                pltpu.make_async_copy(source, target, load_sem.at[used + i])
                for i, (source, target) in enumerate(group)
            ]
        )
        used += len(group)
    for group in loads:
        for copy in group:
            copy.start()

    def arrive(group):
        for copy in loads[group]:
            copy.wait()

    barrier = pltpu.get_barrier_semaphore()
    for peer in x_peers + z_peers:
        pl.semaphore_signal(barrier, inc=1, device_id=peer, device_id_type=MESH)

    lanes = [slice(128 * c, 128 * c + 128) for c in range(4)]
    halves_of = [slice(0, 64), slice(64, 128)]
    lane = lax.broadcasted_iota(jnp.int32, (128, 128), 1)
    at_end = (lane < 8) | (lane >= 120)

    def on_left(name, value):
        return mm(tables[name][...], stack_rows(value))

    def pair(i, j):
        return i if i == j else 2 + i + j

    def flux_of(factor, grads):
        return [
            factor(pair(d, 0)) * grads[0]
            + factor(pair(d, 1)) * grads[1]
            + factor(pair(d, 2)) * grads[2]
            for d in range(3)
        ]

    def end_operator(field):
        packed = jnp.where(
            lane < 16,
            pltpu.roll(field[0], 8, 1),
            jnp.where(lane < 32, pltpu.roll(field[1], 24, 1), pltpu.roll(field[2], 40, 1)),
        )
        lines = mm_right(stack_lanes(packed), tables["to_ends"])
        joined = []
        planar = []
        for e in range(2):
            rows = halves_of[e]
            fine = on_left("xy_interp", lines[rows, 128:])
            grads = on_left("xy_grad", packed[rows])
            flux = flux_of(
                lambda slot: ge_s[slot, e], (grads[:64], grads[64:], lines[rows, :128])
            )
            first = jnp.concatenate([ue_s[d, e] * fine for d in range(2)], axis=0)
            back_12 = on_left("xy_back_12", first)
            back_3 = on_left("xy_back_3", ue_s[2, e] * fine)
            planar.append(on_left("xy_grad_back", jnp.concatenate(flux[:2], axis=0)))
            joined.append(jnp.concatenate([back_12, back_3, flux[2]], axis=1))
        normal = mm_right(stack_lanes(jnp.concatenate(joined, axis=0)), tables["from_ends"])
        return normal + jnp.concatenate(planar, axis=0)

    def stiffness(high, low):
        stacked = jnp.concatenate(
            [jnp.concatenate([high[c], low[c], high[c]], axis=1) for c in range(3)], axis=0
        )
        grad_z = mm_right(stacked, tables["z_grad"])
        planar, fluxes = [], [[None, None] for _ in range(3)]
        for e in range(2):
            wide_high = jnp.concatenate([high[c][halves_of[e]] for c in range(3)], axis=1)
            wide_low = jnp.concatenate([low[c][halves_of[e]] for c in range(3)], axis=1)
            grads = mm(
                tables["xy_grad"][...],
                jnp.concatenate([wide_high, wide_low, wide_high], axis=0),
            )
            flux = [[None] * 3 for _ in range(2)]
            for c in range(3):
                start = 128 * c + 64 * e
                g = (grads[:64, lanes[c]], grads[64:, lanes[c]], grad_z[start : start + 64])
                flux[0][c], flux[1][c], fluxes[c][e] = flux_of(lambda slot: gw_s[slot, e], g)
            joined = jnp.concatenate([jnp.concatenate(f, axis=1) for f in flux], axis=0)
            planar.append(on_left("xy_grad_back", joined))
        normal = mm_right(
            stack_lanes(jnp.concatenate([f for two in fluxes for f in two], axis=0)),
            tables["z_grad_back"],
        )
        return jnp.concatenate(planar, axis=0) + jnp.concatenate(
            [normal[128 * c : 128 * c + 128] for c in range(3)], axis=1
        )

    def middle_convection(field, high, low):
        shifted_high, shifted_low = split(pltpu.roll(field[2], 72, 1))
        stacked = jnp.concatenate(
            [
                jnp.concatenate([high[0], high[2], low[0], low[2], high[0], high[2]], axis=1),
                jnp.concatenate(
                    [high[1], shifted_high, low[1], shifted_low, high[1], shifted_high], axis=1
                ),
            ],
            axis=0,
        )
        both = mm_right(stacked, tables["to_middle"])
        lines = jnp.concatenate([both[:128], both[128:]], axis=1)
        pieces = []
        for e in range(2):
            fine = on_left("xy_interp", lines[halves_of[e]])

            def product(d):
                return jnp.concatenate(
                    [
                        um_s[d, e, :, lanes[k]] * fine[:, lanes[i]]
                        for i, k in enumerate((0, 1, 0, 2))
                    ],
                    axis=1,
                )

            first = jnp.concatenate([product(0), product(1)], axis=0)
            pieces.append((on_left("xy_back_12", first), on_left("xy_back_3", product(2))))
        joined = [
            jnp.concatenate([part[:, 256 * t : 256 * t + 256] for part in pieces[e]], axis=1)
            for t in range(2)
            for e in range(2)
        ]
        back = mm_right(stack_lanes(jnp.concatenate(joined, axis=0)), tables["from_middle"])
        tail = back[:128, 128:] + pltpu.roll(back[128:, 128:], 56, 1)
        return jnp.concatenate([back[:128, :128], back[128:, :128], tail], axis=1)

    def with_ends(value, end_tile):
        return jnp.concatenate(
            [
                jnp.where(at_end, pltpu.roll(end_tile, 120 - 16 * c, 1), value[:, lanes[c]])
                for c in range(3)
            ],
            axis=1,
        )

    def local_sum(value, low, high):
        width, count = value.shape[1], high - low
        two = [value[64 * e + 8 * low : 64 * e + 8 * high] for e in range(2)]
        two = [member.reshape(count, 8, width) for member in two]
        place = lax.broadcasted_iota(jnp.int32, (count, 8, width), 1)
        lane = lax.broadcasted_iota(jnp.int32, (8 * count, 128), 1)
        begins = (lane % 8 == 0) & (lane > 0)
        closes = (lane % 8 == 7) & (lane < 127)
        results = []
        for own, other in ((two[0], two[1]), (two[1], two[0])):
            before = pltpu.roll(other, 1, 1)
            after = pltpu.roll(other, 7, 1)
            total = own + jnp.where(place == 7, after, jnp.where(place == 0, before, 0.0))
            total = total.reshape(8 * count, width)
            pieces = []
            for c in range(width // 128):
                piece = total[:, lanes[c]]
                near = jnp.where(
                    closes,
                    pltpu.roll(piece, 127, 1),
                    jnp.where(begins, pltpu.roll(piece, 1, 1), 0.0),
                )
                pieces.append(piece + near)
            results.append(jnp.concatenate(pieces, axis=1))
        return results

    def picks_of(width, find):
        row = lax.broadcasted_iota(jnp.int32, (8, width), 0)
        lane = lax.broadcasted_iota(jnp.int32, (8, width), 1)
        return find(row, lane).astype(F32).astype(BF16)

    picks_in = picks_of(
        512,
        lambda row, lane: ((row < 4) & (lane == 128 * row))
        | ((row >= 4) & (lane == 128 * (row - 4) + 127)),
    )
    picks_out = picks_of(
        256,
        lambda row, lane: ((row < 3) & (lane == 16 * row + 8))
        | ((row >= 4) & (row < 7) & (lane == 16 * (row - 4) + 7))
        | ((row == 3) & (lane == 128))
        | ((row == 7) & (lane == 255)),
    )
    side = lax.broadcasted_iota(jnp.int32, (8, 128), 0)
    place = lax.broadcasted_iota(jnp.int32, (8, 128), 1) % 64

    def remote(source, target, phase, i, peer):
        return pltpu.make_async_remote_copy(
            src_ref=source,
            dst_ref=target,
            send_sem=send_sem.at[phase, i],
            recv_sem=recv_sem.at[phase, i],
            device_id=peer,
            device_id_type=MESH,
        )

    def send_ends(phase, value, extra_peers):
        high, low = split(value)
        picks = picks_out[:, : value.shape[1]]
        contract = (((1,), (1,)), ((), ()))
        tile = lax.dot_general(
            picks, high, contract, preferred_element_type=F32
        ) + lax.dot_general(picks, low, contract, preferred_element_type=F32)
        after = jnp.where(place % 8 == 7, pltpu.roll(tile, 71, 1), 0.0)
        before = jnp.where(place % 8 == 0, pltpu.roll(tile, 57, 1), 0.0)
        zs[phase] = tile + after + before
        copies = [
            remote(zs.at[phase], zr.at[phase, i], phase, 2 + i, peer)
            for i, peer in enumerate(z_peers)
        ]
        extra = [
            remote(zs.at[phase], dr.at[i], phase, 4 + i, peer)
            for i, peer in enumerate(extra_peers)
        ]
        for copy in extra + copies:
            copy.start()
        return copies, extra

    def exchange(phase, value, xs, xr, z_copies, corner_copies):
        faces = [local_sum(value, 7, 8), local_sum(value, 0, 1)]
        for i in range(2):
            for e in range(2):
                xs[i, 8 * e : 8 * e + 8] = faces[i][e]
        x_copies = [
            remote(xs.at[i], xr.at[i], phase, i, peer) for i, peer in enumerate(x_peers)
        ]
        for copy in x_copies:
            copy.start()
        inner = local_sum(value, 1, 7)
        for copy in z_copies:
            copy.wait_recv()
        from_down = (side >= 4) & (col > 0)
        from_up = (side < 4) & (col < n_col - 1)

        def choose(below, above):
            return jnp.where(from_down, below, jnp.where(from_up, above, 0.0))

        lines = choose(zr[phase, 0], zr[phase, 1])
        if corner_copies:
            others = corner_copies
        else:
            rs[...] = lines
            others = [
                remote(rs, rr.at[i], phase, 4 + i, peer) for i, peer in enumerate(x_peers)
            ]
            for copy in others:
                copy.start()
        for copy in x_copies + others:
            copy.wait_recv()
        if corner_copies:
            beside = (choose(dr[0], dr[1]), choose(dr[2], dr[3]))
        else:
            beside = (rr[0], rr[1])
        lines = lines + jnp.where(place < 8, pltpu.roll(beside[0], 72, 1), 0.0)
        lines = lines + jnp.where(place >= 56, pltpu.roll(beside[1], 56, 1), 0.0)
        lines = pltpu.roll(lines, 4, 0)
        columns = jnp.transpose(jnp.concatenate([lines] * 16, axis=0))[:, :8]
        high, low = split(columns)
        picks = picks_in[:, : value.shape[1]]
        pieces = []
        for e in range(2):
            pieces.append(faces[1][e] + xr[0, 8 * e : 8 * e + 8])
            pieces.append(inner[e])
            pieces.append(faces[0][e] + xr[1, 8 * e : 8 * e + 8])
        total = jnp.concatenate(pieces, axis=0) + (mm(high, picks) + mm(low, picks))
        for copy in x_copies + z_copies + others:
            copy.wait_send()
        return total

    lane_row = lax.broadcasted_iota(jnp.int32, (1, 128), 1)
    wall = ((lane_row == 0) & (col == 0)) | ((lane_row == 127) & (col == n_col - 1))
    interior = jnp.where(wall, 0.0, 1.0).astype(F32)

    arrive(0)
    fine_rows = []
    for e in range(2):
        rows = jnp.concatenate([b_s[d, e].reshape(64, 128) for d in range(3)], axis=1)
        fine = on_left("xy_interp", rows)
        fine_rows.extend(fine[:, lanes[d]] for d in range(3))
    fine_rows = stack_lanes(jnp.concatenate(fine_rows, axis=0))
    fine_weights = tables["sigma_xy"][:, :1] * tables["sigma_z"][:1]
    flow = mm_right(fine_rows, tables["flow_ends"])
    for e in range(2):
        for d in range(3):
            first = 144 * (3 * e + d)
            ue_s[d, e] = flow[first : first + 144] * fine_weights[:, lanes[0]]

    weights = VISCOSITY * tables["node_weights"][...]
    end_weights = jnp.where(
        lane[:64] < 16,
        pltpu.roll(weights, 8, 1),
        jnp.where(lane[:64] < 32, pltpu.roll(weights, 24, 1), pltpu.roll(weights, 40, 1)),
    )
    factors = []
    for name in (md_s, mc_s):
        for i in range(3):
            plane = name[i].astype(F32)
            for e in range(2):
                factors.append(plane[:, 8 * e : 8 * e + 8, :].reshape(64, 128))
    end_factors = mm(
        jnp.concatenate(factors, axis=0).astype(BF16), tables["choose_ends"][...]
    )
    for i, factor in enumerate(factors):
        ge_s[i // 2, i % 2] = end_factors[64 * i : 64 * i + 64] * end_weights
        gw_s[i // 2, i % 2] = factor * weights

    start = [v_s[c].reshape(128, 128) for c in range(3)]
    arrive(1)
    end_tile = end_operator(start)
    mass = jnp.concatenate(
        [j_s[e].reshape(64, 128) * tables["node_weights"][...] for e in range(2)], axis=0
    )
    pl.semaphore_wait(barrier, 4)
    z_copies, corner_copies = send_ends(0, jnp.concatenate([end_tile, mass], axis=1), ())

    arrive(2)
    flow = mm_right(fine_rows, tables["flow_middle"])
    for e in range(2):
        for d in range(3):
            first = 144 * (3 * e + d)
            um_s[d, e] = flow[first : first + 144] * fine_weights[:, 128:]

    pairs = [split(member) for member in start]
    high, low = [p[0] for p in pairs], [p[1] for p in pairs]
    value = middle_convection(start, high, low) + stiffness(high, low)
    value = jnp.concatenate([with_ends(value, end_tile), mass], axis=1)
    total = exchange(0, value, xs0, xr0, z_copies, corner_copies)
    inverse = 1.0 / total[:, lanes[3]]
    half = [
        interior * (start[c] - (0.5 * STEP_SIZE) * inverse * total[:, lanes[c]]) for c in range(3)
    ]

    end_tile = end_operator(half)
    z_copies, corner_copies = send_ends(1, end_tile, corner_peers)
    pairs = [split(member) for member in half]
    high, low = [p[0] for p in pairs], [p[1] for p in pairs]
    value = middle_convection(half, high, low) + stiffness(high, low)
    value = with_ends(value, end_tile)
    total = exchange(1, value, xs1, xr1, z_copies, corner_copies)
    for c in range(3):
        result = interior * (
            v_s[c].reshape(128, 128) - STEP_SIZE * inverse * total[:, lanes[c]]
        )
        for e in range(2):
            out[c, :, 8 * e : 8 * e + 8, :] = result[halves_of[e]].reshape(8, 8, 128)


def local(n_span, n_col, adjoint_field, base_flow, metric_diag, metric_cross, jacobian):
    tables = operator_tables()
    table_scratch = [
        pltpu.VMEM(member.shape, jnp.dtype(member.dtype)) for member in tables.values()
    ]
    return pl.pallas_call(
        functools.partial(kernel, n_span, n_col, tuple(tables)),
        out_shape=pltpu.VMEM(adjoint_field.shape, F32),
        in_specs=[pl.BlockSpec(memory_space=pl.ANY)] * (5 + len(tables)),
        out_specs=pl.BlockSpec(memory_space=pltpu.VMEM),
        scratch_shapes=[
            pltpu.VMEM((3, 2, 8, 8, 128), F32),
            pltpu.VMEM((3, 2, 8, 8, 128), F32),
            pltpu.VMEM((2, 8, 8, 128), F32),
            pltpu.VMEM((3, 8, 16, 128), BF16),
            pltpu.VMEM((3, 8, 16, 128), BF16),
            *table_scratch,
            pltpu.VMEM((3, 2, 144, 128), F32),
            pltpu.VMEM((3, 2, 144, 384), F32),
            pltpu.VMEM((6, 2, 64, 128), F32),
            pltpu.VMEM((6, 2, 64, 128), F32),
            pltpu.VMEM((2, 16, 512), F32),
            pltpu.VMEM((2, 16, 512), F32),
            pltpu.VMEM((2, 16, 384), F32),
            pltpu.VMEM((2, 16, 384), F32),
            pltpu.VMEM((2, 8, 128), F32),
            pltpu.VMEM((2, 2, 8, 128), F32),
            pltpu.VMEM((8, 128), F32),
            pltpu.VMEM((2, 8, 128), F32),
            pltpu.VMEM((4, 8, 128), F32),
            pltpu.SemaphoreType.DMA((8 + len(tables),)),
            pltpu.SemaphoreType.DMA((2, 8)),
            pltpu.SemaphoreType.DMA((2, 8)),
        ],
        compiler_params=pltpu.CompilerParams(collective_id=0, has_side_effects=True),
    )(
        adjoint_field,
        base_flow,
        metric_diag,
        metric_cross,
        jacobian,
        *[jnp.asarray(member) for member in tables.values()],
    )


def solution(mesh):
    in_specs = (
        P(None, "span", None, "col"),
        P(None, "span", None, "col"),
        P(None, "span", None, "col"),
        P(None, "span", None, "col"),
        P("span", None, "col"),
    )
    out_specs = P(None, "span", None, "col")
    body = functools.partial(local, mesh.shape["span"], mesh.shape["col"])
    return jax.shard_map(body, mesh=mesh, in_specs=in_specs, out_specs=out_specs, check_vma=False)
```

```python
import functools

import jax
import jax.numpy as jnp
import ml_dtypes
import numpy as np
from jax import lax
from jax.experimental import pallas as pl
from jax.experimental.pallas import tpu as pltpu
from jax.sharding import PartitionSpec as P

VISCOSITY = 0.05
STEP_SIZE = 0.01
GLL_INNER = [
    -0.8717401485096066,
    -0.5917001814331423,
    -0.2092992179024789,
    0.2092992179024789,
    0.5917001814331423,
    0.8717401485096066,
]
GAUSS_POINTS = [
    -0.9815606342467192,
    -0.9041172563704749,
    -0.7699026741943047,
    -0.5873179542866175,
    -0.3678314989981802,
    -0.1252334085114689,
    0.1252334085114689,
    0.3678314989981802,
    0.5873179542866175,
    0.7699026741943047,
    0.9041172563704749,
    0.9815606342467192,
]
GAUSS_WEIGHTS = [
    0.0471753363865118,
    0.1069393259953184,
    0.1600783285433462,
    0.2031674267230659,
    0.2334925365383548,
    0.2491470458134028,
    0.2491470458134028,
    0.2334925365383548,
    0.2031674267230659,
    0.1600783285433462,
    0.1069393259953184,
    0.0471753363865118,
]
MESH = pl.DeviceIdType.MESH
F32 = jnp.float32
BF16 = jnp.bfloat16


def legendre_seven(points):
    previous = points * 0.0 + 1.0
    current = points
    for degree in range(1, 7):
        following = ((2.0 * degree + 1.0) * points * current - degree * previous) / (degree + 1.0)
        previous = current
        current = following
    return current


def node_tables():
    gll_nodes = np.array([-1.0] + GLL_INNER + [1.0])
    values = legendre_seven(gll_nodes)
    node_weights = 2.0 / (56.0 * values * values)
    identity = np.eye(8, dtype=bool)
    spacing = gll_nodes[:, None] - gll_nodes[None, :]
    derivative = np.where(
        identity, 0.0, values[:, None] / (values[None, :] * np.where(identity, 1.0, spacing))
    )
    corner_terms = np.concatenate([np.array([-14.0]), np.zeros(6), np.array([14.0])])
    derivative = derivative + np.eye(8) * corner_terms[None, :]
    gauss_nodes = np.array(GAUSS_POINTS)
    gauss_weights = np.array(GAUSS_WEIGHTS)
    numerators = gauss_nodes[:, None, None] - gll_nodes[None, None, :]
    denominators = np.where(identity, 1.0, spacing)[None]
    ratios = np.where(identity[None], 1.0, numerators / denominators)
    interpolation = ratios.prod(axis=2)
    slope_interp = interpolation @ derivative
    return tuple(
        np.asarray(member, np.float32).astype(np.float64)
        for member in (derivative, node_weights, interpolation, slope_interp, gauss_weights)
    )


def halves(matrix):
    high = matrix.astype(np.float32).astype(ml_dtypes.bfloat16)
    low = (matrix - high.astype(np.float64)).astype(np.float32).astype(ml_dtypes.bfloat16)
    return high, low


def left_table(matrix):
    return np.concatenate([halves(matrix)[i] for i in (0, 0, 1)], axis=1)


def right_table(matrix):
    return np.stack(halves(matrix))


def operator_tables():
    dm, rho, jm, dj, sigma = node_tables()
    eye8, eye16 = np.eye(8), np.eye(16)
    ends = [(16 * c + 8 * s, 24 * c + 12 * s) for c in range(3) for s in range(2)]
    middle = [(8 * a, 12 * (a - 1)) for a in range(1, 15)]
    middle += [(128 + 8 * a, 12 * (13 + a)) for a in range(1, 8)]

    def blocks(matrix, places, rows, columns):
        table = np.zeros((rows, columns))
        for first, second in places:
            height, width = matrix.shape
            second = second if width == 12 else first
            table[first : first + height, second : second + width] = matrix
        return table

    to_ends = np.concatenate(
        [blocks(dm.T, ends, 128, 128), blocks(jm.T, ends, 128, 128)], axis=1
    )
    from_ends = np.concatenate(
        [
            blocks(jm.T, ends, 128, 128).T,
            blocks(dj.T, ends, 128, 128).T,
            blocks(dm.T, ends, 128, 128).T,
        ],
        axis=0,
    )
    to_middle = blocks(jm.T, middle, 256, 256)
    from_middle = np.concatenate([to_middle.T, blocks(dj.T, middle, 256, 256).T], axis=0)

    flow_ends, flow_middle = np.zeros((128, 128)), np.zeros((128, 512))
    sigma_z = np.zeros((1, 512))
    for node, gauss in ends:
        element = 0 if node % 16 == 8 else 120
        flow_ends[element : element + 8, gauss : gauss + 12] = jm.T
        sigma_z[0, gauss : gauss + 12] = sigma
    for t in range(2):
        for node, gauss in middle:
            element = node if node < 128 else node - 128 + 56 * t
            flow_middle[element : element + 8, 256 * t + gauss : 256 * t + gauss + 12] = jm.T
    tile = np.zeros(256)
    for node, gauss in middle:
        tile[gauss : gauss + 12] = sigma
    sigma_z[0, 128:256], sigma_z[0, 256:384], sigma_z[0, 384:] = tile[:128], tile[128:], tile[128:]
    flow_middle = np.concatenate([flow_middle[:, :256], flow_middle[:, 384:]], axis=1)
    sigma_z = np.broadcast_to(sigma_z, (8, 512)).astype(np.float32)
    sigma_xy = np.broadcast_to(np.kron(sigma, sigma)[:, None], (144, 128)).astype(np.float32)

    node_weights = (np.kron(rho, rho)[:, None] * np.tile(rho, 16)[None, :]).astype(np.float32)
    choose_ends = np.zeros((128, 128))
    for node, _ in ends:
        element = 0 if node % 16 == 8 else 120
        choose_ends[element : element + 8, node : node + 8] = np.eye(8)
    return {
        "z_grad": right_table(np.kron(eye16, dm.T)),
        "z_grad_back": right_table(np.kron(eye16, dm)),
        "xy_grad": left_table(np.concatenate([np.kron(dm, eye8), np.kron(eye8, dm)], axis=0)),
        "xy_grad_back": left_table(
            np.concatenate([np.kron(dm.T, eye8), np.kron(eye8, dm.T)], axis=1)
        ),
        "xy_interp": left_table(np.kron(jm, jm)),
        "xy_back_12": left_table(
            np.concatenate([np.kron(dj.T, jm.T), np.kron(jm.T, dj.T)], axis=1)
        ),
        "xy_back_3": left_table(np.kron(jm.T, jm.T)),
        "to_ends": right_table(to_ends),
        "from_ends": right_table(from_ends),
        "to_middle": right_table(to_middle),
        "from_middle": right_table(from_middle),
        "flow_ends": right_table(flow_ends),
        "flow_middle": right_table(flow_middle),
        "choose_ends": choose_ends.astype(ml_dtypes.bfloat16),
        "sigma_xy": sigma_xy,
        "sigma_z": sigma_z,
        "node_weights": node_weights,
    }


def split(value):
    high = value.astype(BF16)
    low = (value - high.astype(F32)).astype(BF16)
    return high, low


def mm(a, b):
    return jnp.dot(a, b, preferred_element_type=F32)


def mm_right(stacked, table):
    return mm(stacked, jnp.concatenate([table[0], table[0], table[1]], axis=0))


def stack_rows(value):
    high, low = split(value)
    return jnp.concatenate([high, low, high], axis=0)


def stack_lanes(value):
    high, low = split(value)
    return jnp.concatenate([high, low, high], axis=1)


def kernel(n_span, n_col, names, *refs):
    n_tables = len(names)
    (adj_h, base_h, md_h, mc_h, jac_h) = refs[:5]
    tables_h = dict(zip(names, refs[5 : 5 + n_tables]))
    out = refs[5 + n_tables]
    refs = refs[6 + n_tables :]
    (v_s, b_s, j_s, md_s, mc_s) = refs[:5]
    tables = dict(zip(names, refs[5 : 5 + n_tables]))
    refs = refs[5 + n_tables :]
    (ue_s, um_s, ge_s, gw_s, xs0, xr0, xs1, xr1, zs, zr, cr) = refs[:11]
    (load_sem, send_sem, recv_sem) = refs[11:]

    span = lax.axis_index("span")
    col = lax.axis_index("col")
    right, left = lax.rem(span + 1, n_span), lax.rem(span + n_span - 1, n_span)
    up, down = lax.rem(col + 1, n_col), lax.rem(col + n_col - 1, n_col)
    x_peers = ((right, col), (left, col))
    has_up, has_down = col < n_col - 1, col > 0

    table = {name: (tables_h[name], tables[name]) for name in names}
    groups = [
        [(base_h, b_s)]
        + [table[n] for n in ("xy_interp", "flow_ends", "sigma_xy", "sigma_z")]
        + [(md_h, md_s), (mc_h, mc_s)]
        + [(adj_h, v_s)]
        + [table[n] for n in ("choose_ends", "node_weights", "to_ends", "xy_grad")],
        [table[n] for n in ("xy_grad_back", "xy_back_12", "xy_back_3", "from_ends")]
        + [(jac_h, j_s)],
        [table[n] for n in ("z_grad", "z_grad_back", "flow_middle", "to_middle", "from_middle")],
    ]
    loads, used = [], 0
    for group in groups:
        loads.append(
            [
                pltpu.make_async_copy(source, target, load_sem.at[used + i])
                for i, (source, target) in enumerate(group)
            ]
        )
        used += len(group)
    for group in loads:
        for copy in group:
            copy.start()

    def arrive(group):
        for copy in loads[group]:
            copy.wait()

    barrier = pltpu.get_barrier_semaphore()

    def greet(peers):
        for peer in peers:
            pl.semaphore_signal(barrier, inc=1, device_id=peer, device_id_type=MESH)

    greet(x_peers)
    pl.when(has_up)(lambda: greet(((span, up), (right, up))))
    pl.when(has_down)(lambda: greet(((span, down), (left, down))))

    def await_peers():
        inside = has_up & has_down
        pl.when(inside)(lambda: pl.semaphore_wait(barrier, 6))
        pl.when(jnp.logical_not(inside))(lambda: pl.semaphore_wait(barrier, 4))

    lanes = [slice(128 * c, 128 * c + 128) for c in range(4)]
    halves_of = [slice(0, 64), slice(64, 128)]
    lane = lax.broadcasted_iota(jnp.int32, (128, 128), 1)
    at_end = (lane < 8) | (lane >= 120)

    def on_left(name, value):
        return mm(tables[name][...], stack_rows(value))

    def pair(i, j):
        return i if i == j else 2 + i + j

    def flux_of(factor, grads):
        return [
            factor(pair(d, 0)) * grads[0]
            + factor(pair(d, 1)) * grads[1]
            + factor(pair(d, 2)) * grads[2]
            for d in range(3)
        ]

    def end_operator(field):
        packed = jnp.where(
            lane < 16,
            pltpu.roll(field[0], 8, 1),
            jnp.where(lane < 32, pltpu.roll(field[1], 24, 1), pltpu.roll(field[2], 40, 1)),
        )
        lines = mm_right(stack_lanes(packed), tables["to_ends"])
        joined = []
        planar = []
        for e in range(2):
            rows = halves_of[e]
            fine = on_left("xy_interp", lines[rows, 128:])
            grads = on_left("xy_grad", packed[rows])
            flux = flux_of(
                lambda slot: ge_s[slot, e], (grads[:64], grads[64:], lines[rows, :128])
            )
            first = jnp.concatenate([ue_s[d, e] * fine for d in range(2)], axis=0)
            back_12 = on_left("xy_back_12", first)
            back_3 = on_left("xy_back_3", ue_s[2, e] * fine)
            planar.append(on_left("xy_grad_back", jnp.concatenate(flux[:2], axis=0)))
            joined.append(jnp.concatenate([back_12, back_3, flux[2]], axis=1))
        normal = mm_right(stack_lanes(jnp.concatenate(joined, axis=0)), tables["from_ends"])
        return normal + jnp.concatenate(planar, axis=0)

    def stiffness(high, low):
        stacked = jnp.concatenate(
            [jnp.concatenate([high[c], low[c], high[c]], axis=1) for c in range(3)], axis=0
        )
        grad_z = mm_right(stacked, tables["z_grad"])
        planar, fluxes = [], [[None, None] for _ in range(3)]
        for e in range(2):
            wide_high = jnp.concatenate([high[c][halves_of[e]] for c in range(3)], axis=1)
            wide_low = jnp.concatenate([low[c][halves_of[e]] for c in range(3)], axis=1)
            grads = mm(
                tables["xy_grad"][...],
                jnp.concatenate([wide_high, wide_low, wide_high], axis=0),
            )
            flux = [[None] * 3 for _ in range(2)]
            for c in range(3):
                start = 128 * c + 64 * e
                g = (grads[:64, lanes[c]], grads[64:, lanes[c]], grad_z[start : start + 64])
                flux[0][c], flux[1][c], fluxes[c][e] = flux_of(lambda slot: gw_s[slot, e], g)
            joined = jnp.concatenate([jnp.concatenate(f, axis=1) for f in flux], axis=0)
            planar.append(on_left("xy_grad_back", joined))
        normal = mm_right(
            stack_lanes(jnp.concatenate([f for two in fluxes for f in two], axis=0)),
            tables["z_grad_back"],
        )
        return jnp.concatenate(planar, axis=0) + jnp.concatenate(
            [normal[128 * c : 128 * c + 128] for c in range(3)], axis=1
        )

    def middle_convection(field, high, low):
        shifted_high, shifted_low = split(pltpu.roll(field[2], 72, 1))
        stacked = jnp.concatenate(
            [
                jnp.concatenate([high[0], high[2], low[0], low[2], high[0], high[2]], axis=1),
                jnp.concatenate(
                    [high[1], shifted_high, low[1], shifted_low, high[1], shifted_high], axis=1
                ),
            ],
            axis=0,
        )
        both = mm_right(stacked, tables["to_middle"])
        lines = jnp.concatenate([both[:128], both[128:]], axis=1)
        pieces = []
        for e in range(2):
            fine = on_left("xy_interp", lines[halves_of[e]])

            def product(d):
                return jnp.concatenate(
                    [
                        um_s[d, e, :, lanes[k]] * fine[:, lanes[i]]
                        for i, k in enumerate((0, 1, 0, 2))
                    ],
                    axis=1,
                )

            first = jnp.concatenate([product(0), product(1)], axis=0)
            pieces.append((on_left("xy_back_12", first), on_left("xy_back_3", product(2))))
        joined = [
            jnp.concatenate([part[:, 256 * t : 256 * t + 256] for part in pieces[e]], axis=1)
            for t in range(2)
            for e in range(2)
        ]
        back = mm_right(stack_lanes(jnp.concatenate(joined, axis=0)), tables["from_middle"])
        tail = back[:128, 128:] + pltpu.roll(back[128:, 128:], 56, 1)
        return jnp.concatenate([back[:128, :128], back[128:, :128], tail], axis=1)

    def with_ends(value, end_tile):
        return jnp.concatenate(
            [
                jnp.where(at_end, pltpu.roll(end_tile, 120 - 16 * c, 1), value[:, lanes[c]])
                for c in range(3)
            ],
            axis=1,
        )

    def local_sum(value, low, high):
        width, count = value.shape[1], high - low
        two = [value[64 * e + 8 * low : 64 * e + 8 * high] for e in range(2)]
        two = [member.reshape(count, 8, width) for member in two]
        place = lax.broadcasted_iota(jnp.int32, (count, 8, width), 1)
        lane = lax.broadcasted_iota(jnp.int32, (8 * count, 128), 1)
        begins = (lane % 8 == 0) & (lane > 0)
        closes = (lane % 8 == 7) & (lane < 127)
        results = []
        for own, other in ((two[0], two[1]), (two[1], two[0])):
            before = pltpu.roll(other, 1, 1)
            after = pltpu.roll(other, 7, 1)
            total = own + jnp.where(place == 7, after, jnp.where(place == 0, before, 0.0))
            total = total.reshape(8 * count, width)
            pieces = []
            for c in range(width // 128):
                piece = total[:, lanes[c]]
                near = jnp.where(
                    closes,
                    pltpu.roll(piece, 127, 1),
                    jnp.where(begins, pltpu.roll(piece, 1, 1), 0.0),
                )
                pieces.append(piece + near)
            results.append(jnp.concatenate(pieces, axis=1))
        return results

    def picks_of(width, find):
        row = lax.broadcasted_iota(jnp.int32, (8, width), 0)
        lane = lax.broadcasted_iota(jnp.int32, (8, width), 1)
        return find(row, lane).astype(F32).astype(BF16)

    picks_out = picks_of(
        256,
        lambda row, lane: ((row < 3) & (lane == 16 * row + 8))
        | ((row >= 4) & (row < 7) & (lane == 16 * (row - 4) + 7))
        | ((row == 3) & (lane == 128))
        | ((row == 7) & (lane == 255)),
    )
    side = lax.broadcasted_iota(jnp.int32, (8, 128), 0)
    place = lax.broadcasted_iota(jnp.int32, (8, 128), 1) % 64

    def remote(source, target, phase, i, peer):
        return pltpu.make_async_remote_copy(
            src_ref=source,
            dst_ref=target,
            send_sem=send_sem.at[phase, i],
            recv_sem=recv_sem.at[phase, i],
            device_id=peer,
            device_id_type=MESH,
        )

    def send_ends(phase, value):
        high, low = split(value)
        picks = picks_out[:, : value.shape[1]]
        contract = (((1,), (1,)), ((), ()))
        tile = lax.dot_general(
            picks, high, contract, preferred_element_type=F32
        ) + lax.dot_general(picks, low, contract, preferred_element_type=F32)
        after = jnp.where(place % 8 == 7, pltpu.roll(tile, 71, 1), 0.0)
        before = jnp.where(place % 8 == 0, pltpu.roll(tile, 57, 1), 0.0)
        zs[phase] = tile + after + before
        tile = zs.at[phase]
        copies = [
            (remote(tile, zr.at[phase, 0], phase, 2, (span, up)), has_up, has_down),
            (remote(tile, zr.at[phase, 1], phase, 3, (span, down)), has_down, has_up),
            (remote(tile, cr.at[phase, 0], phase, 4, (right, up)), has_up, has_down),
            (remote(tile, cr.at[phase, 3], phase, 7, (left, down)), has_down, has_up),
        ]
        if phase == 1:
            copies += [
                (remote(tile, cr.at[phase, 1], phase, 5, (right, down)), has_down, has_up),
                (remote(tile, cr.at[phase, 2], phase, 6, (left, up)), has_up, has_down),
            ]
        for copy, sends, _ in copies:
            pl.when(sends)(copy.start)
        return copies

    sent = []

    def exchange(phase, value, xs, xr, copies):
        faces = [local_sum(value, 7, 8), local_sum(value, 0, 1)]
        for i in range(2):
            for e in range(2):
                xs[i, 8 * e : 8 * e + 8] = faces[i][e]
        x_copies = [
            remote(xs.at[i], xr.at[i], phase, i, peer) for i, peer in enumerate(x_peers)
        ]
        for copy in x_copies:
            copy.start()
        inner = local_sum(value, 1, 7)
        if phase == 0:
            relays = [
                (remote(zr.at[0, 1], cr.at[0, 1], 0, 5, (right, col)), has_up, has_up),
                (remote(zr.at[0, 0], cr.at[0, 2], 0, 6, (left, col)), has_down, has_down),
            ]
            def forward(order):
                for k in order:
                    pl.when(copies[1 - k][2])(copies[1 - k][0].wait_recv)
                    pl.when(relays[k][1])(relays[k][0].start)

            pl.when(col % 2 == 0)(lambda: forward((0, 1)))
            pl.when(col % 2 == 1)(lambda: forward((1, 0)))
            pending = copies[2:] + relays
            all_copies = copies + relays
        else:
            pending = all_copies = copies
        for copy, _, receives in pending:
            pl.when(receives)(copy.wait_recv)
        for copy in x_copies:
            copy.wait_recv()
        from_down = (side >= 4) & has_down
        from_up = (side < 4) & has_up

        def choose(below, above):
            return jnp.where(from_down, below, jnp.where(from_up, above, 0.0))

        lines = choose(zr[phase, 0], zr[phase, 1])
        beside = (choose(cr[phase, 0], cr[phase, 1]), choose(cr[phase, 2], cr[phase, 3]))
        lines = lines + jnp.where(place < 8, pltpu.roll(beside[0], 72, 1), 0.0)
        lines = lines + jnp.where(place >= 56, pltpu.roll(beside[1], 56, 1), 0.0)
        lines = pltpu.roll(lines, 4, 0)
        columns = jnp.transpose(lines)
        added = jnp.concatenate(
            [
                jnp.where(
                    lane == 0,
                    columns[:, c : c + 1],
                    jnp.where(lane == 127, columns[:, 4 + c : 5 + c], 0.0),
                )
                for c in range(value.shape[1] // 128)
            ],
            axis=1,
        )
        pieces = []
        for e in range(2):
            pieces.append(faces[1][e] + xr[0, 8 * e : 8 * e + 8])
            pieces.append(inner[e])
            pieces.append(faces[0][e] + xr[1, 8 * e : 8 * e + 8])
        total = jnp.concatenate(pieces, axis=0) + added
        sent.extend([(copy, True) for copy in x_copies] + [c[:2] for c in all_copies])
        return total

    lane_row = lax.broadcasted_iota(jnp.int32, (1, 128), 1)
    wall = ((lane_row == 0) & (col == 0)) | ((lane_row == 127) & (col == n_col - 1))
    interior = jnp.where(wall, 0.0, 1.0).astype(F32)

    arrive(0)
    fine_rows = []
    for e in range(2):
        rows = jnp.concatenate([b_s[d, :, 8 * e : 8 * e + 8, :].reshape(64, 128) for d in range(3)], axis=1)
        fine = on_left("xy_interp", rows)
        fine_rows.extend(fine[:, lanes[d]] for d in range(3))
    fine_rows = stack_lanes(jnp.concatenate(fine_rows, axis=0))
    fine_weights = tables["sigma_xy"][:, :1] * tables["sigma_z"][:1]
    flow = mm_right(fine_rows, tables["flow_ends"])
    for e in range(2):
        for d in range(3):
            first = 144 * (3 * e + d)
            ue_s[d, e] = flow[first : first + 144] * fine_weights[:, lanes[0]]

    weights = VISCOSITY * tables["node_weights"][...]
    end_weights = jnp.where(
        lane[:64] < 16,
        pltpu.roll(weights, 8, 1),
        jnp.where(lane[:64] < 32, pltpu.roll(weights, 24, 1), pltpu.roll(weights, 40, 1)),
    )
    factors = []
    for name in (md_s, mc_s):
        for i in range(3):
            plane = name[i].astype(F32)
            for e in range(2):
                factors.append(plane[:, 8 * e : 8 * e + 8, :].reshape(64, 128))
    end_factors = mm(
        jnp.concatenate(factors, axis=0).astype(BF16), tables["choose_ends"][...]
    )
    for i, factor in enumerate(factors):
        ge_s[i // 2, i % 2] = end_factors[64 * i : 64 * i + 64] * end_weights
        gw_s[i // 2, i % 2] = factor * weights

    def field_of(c):
        return jnp.concatenate(
            [v_s[c, :, 8 * e : 8 * e + 8, :].reshape(64, 128) for e in range(2)], axis=0
        )

    start = [field_of(c) for c in range(3)]
    arrive(1)
    end_tile = end_operator(start)
    mass = jnp.concatenate(
        [j_s[:, 8 * e : 8 * e + 8, :].reshape(64, 128) * tables["node_weights"][...] for e in range(2)], axis=0
    )

    arrive(2)
    flow = mm_right(fine_rows, tables["flow_middle"])
    for e in range(2):
        for d in range(3):
            first = 144 * (3 * e + d)
            um_s[d, e] = flow[first : first + 144] * fine_weights[:, 128:]

    pairs = [split(member) for member in start]
    high, low = [p[0] for p in pairs], [p[1] for p in pairs]
    value = middle_convection(start, high, low)
    value = value + stiffness(high, low)
    await_peers()
    copies = send_ends(0, jnp.concatenate([end_tile, mass], axis=1))
    value = jnp.concatenate([with_ends(value, end_tile), mass], axis=1)
    total = exchange(0, value, xs0, xr0, copies)
    inverse = 1.0 / total[:, lanes[3]]
    half = [
        interior * (start[c] - (0.5 * STEP_SIZE) * inverse * total[:, lanes[c]]) for c in range(3)
    ]

    end_tile = end_operator(half)
    copies = send_ends(1, end_tile)
    pairs = [split(member) for member in half]
    high, low = [p[0] for p in pairs], [p[1] for p in pairs]
    value = middle_convection(half, high, low) + stiffness(high, low)
    value = with_ends(value, end_tile)
    total = exchange(1, value, xs1, xr1, copies)
    for c in range(3):
        result = interior * (
            field_of(c) - STEP_SIZE * inverse * total[:, lanes[c]]
        )
        for e in range(2):
            out[c, :, 8 * e : 8 * e + 8, :] = result[halves_of[e]].reshape(8, 8, 128)
    for copy, sends in sent:
        if sends is True:
            copy.wait_send()
        else:
            pl.when(sends)(copy.wait_send)


def local(n_span, n_col, adjoint_field, base_flow, metric_diag, metric_cross, jacobian):
    tables = operator_tables()
    table_scratch = [
        pltpu.VMEM(member.shape, jnp.dtype(member.dtype)) for member in tables.values()
    ]
    return pl.pallas_call(
        functools.partial(kernel, n_span, n_col, tuple(tables)),
        out_shape=pltpu.VMEM(adjoint_field.shape, F32),
        in_specs=[pl.BlockSpec(memory_space=pl.ANY)] * (5 + len(tables)),
        out_specs=pl.BlockSpec(memory_space=pltpu.VMEM),
        scratch_shapes=[
            pltpu.VMEM((3, 8, 16, 128), F32),
            pltpu.VMEM((3, 8, 16, 128), F32),
            pltpu.VMEM((8, 16, 128), F32),
            pltpu.VMEM((3, 8, 16, 128), BF16),
            pltpu.VMEM((3, 8, 16, 128), BF16),
            *table_scratch,
            pltpu.VMEM((3, 2, 144, 128), F32),
            pltpu.VMEM((3, 2, 144, 384), F32),
            pltpu.VMEM((6, 2, 64, 128), F32),
            pltpu.VMEM((6, 2, 64, 128), F32),
            pltpu.VMEM((2, 16, 512), F32),
            pltpu.VMEM((2, 16, 512), F32),
            pltpu.VMEM((2, 16, 384), F32),
            pltpu.VMEM((2, 16, 384), F32),
            pltpu.VMEM((2, 8, 128), F32),
            pltpu.VMEM((2, 2, 8, 128), F32),
            pltpu.VMEM((2, 4, 8, 128), F32),
            pltpu.SemaphoreType.DMA((5 + len(tables),)),
            pltpu.SemaphoreType.DMA((2, 8)),
            pltpu.SemaphoreType.DMA((2, 8)),
        ],
        compiler_params=pltpu.CompilerParams(collective_id=0, has_side_effects=True),
    )(
        adjoint_field,
        base_flow,
        metric_diag,
        metric_cross,
        jacobian,
        *[jnp.asarray(member) for member in tables.values()],
    )


def solution(mesh):
    in_specs = (
        P(None, "span", None, "col"),
        P(None, "span", None, "col"),
        P(None, "span", None, "col"),
        P(None, "span", None, "col"),
        P("span", None, "col"),
    )
    out_specs = P(None, "span", None, "col")
    body = functools.partial(local, mesh.shape["span"], mesh.shape["col"])
    return jax.shard_map(body, mesh=mesh, in_specs=in_specs, out_specs=out_specs, check_vma=False)
```

```python
import functools

import jax
import jax.numpy as jnp
import ml_dtypes
import numpy as np
from jax import lax
from jax.experimental import pallas as pl
from jax.experimental.pallas import tpu as pltpu
from jax.sharding import PartitionSpec as P

VISCOSITY = 0.05
STEP_SIZE = 0.01
GLL_INNER = [
    -0.8717401485096066,
    -0.5917001814331423,
    -0.2092992179024789,
    0.2092992179024789,
    0.5917001814331423,
    0.8717401485096066,
]
GAUSS_POINTS = [
    -0.9815606342467192,
    -0.9041172563704749,
    -0.7699026741943047,
    -0.5873179542866175,
    -0.3678314989981802,
    -0.1252334085114689,
    0.1252334085114689,
    0.3678314989981802,
    0.5873179542866175,
    0.7699026741943047,
    0.9041172563704749,
    0.9815606342467192,
]
GAUSS_WEIGHTS = [
    0.0471753363865118,
    0.1069393259953184,
    0.1600783285433462,
    0.2031674267230659,
    0.2334925365383548,
    0.2491470458134028,
    0.2491470458134028,
    0.2334925365383548,
    0.2031674267230659,
    0.1600783285433462,
    0.1069393259953184,
    0.0471753363865118,
]
MESH = pl.DeviceIdType.MESH
F32 = jnp.float32
BF16 = jnp.bfloat16


def legendre_seven(points):
    previous = points * 0.0 + 1.0
    current = points
    for degree in range(1, 7):
        following = ((2.0 * degree + 1.0) * points * current - degree * previous) / (degree + 1.0)
        previous = current
        current = following
    return current


def node_tables():
    gll_nodes = np.array([-1.0] + GLL_INNER + [1.0])
    values = legendre_seven(gll_nodes)
    node_weights = 2.0 / (56.0 * values * values)
    identity = np.eye(8, dtype=bool)
    spacing = gll_nodes[:, None] - gll_nodes[None, :]
    derivative = np.where(
        identity, 0.0, values[:, None] / (values[None, :] * np.where(identity, 1.0, spacing))
    )
    corner_terms = np.concatenate([np.array([-14.0]), np.zeros(6), np.array([14.0])])
    derivative = derivative + np.eye(8) * corner_terms[None, :]
    gauss_nodes = np.array(GAUSS_POINTS)
    gauss_weights = np.array(GAUSS_WEIGHTS)
    numerators = gauss_nodes[:, None, None] - gll_nodes[None, None, :]
    denominators = np.where(identity, 1.0, spacing)[None]
    ratios = np.where(identity[None], 1.0, numerators / denominators)
    interpolation = ratios.prod(axis=2)
    slope_interp = interpolation @ derivative
    return tuple(
        np.asarray(member, np.float32).astype(np.float64)
        for member in (derivative, node_weights, interpolation, slope_interp, gauss_weights)
    )


def halves(matrix):
    high = matrix.astype(np.float32).astype(ml_dtypes.bfloat16)
    low = (matrix - high.astype(np.float64)).astype(np.float32).astype(ml_dtypes.bfloat16)
    return high, low


def left_table(matrix):
    return np.concatenate([halves(matrix)[i] for i in (0, 0, 1)], axis=1)


def right_table(matrix):
    return np.stack(halves(matrix))


def operator_tables():
    dm, rho, jm, dj, sigma = node_tables()
    eye8, eye16 = np.eye(8), np.eye(16)
    ends = [(16 * c + 8 * s, 24 * c + 12 * s) for c in range(3) for s in range(2)]
    middle = [(8 * a, 12 * (a - 1)) for a in range(1, 15)]
    middle += [(128 + 8 * a, 12 * (13 + a)) for a in range(1, 8)]

    def blocks(matrix, places, rows, columns):
        table = np.zeros((rows, columns))
        for first, second in places:
            height, width = matrix.shape
            second = second if width == 12 else first
            table[first : first + height, second : second + width] = matrix
        return table

    to_ends = np.concatenate(
        [blocks(dm.T, ends, 128, 128), blocks(jm.T, ends, 128, 128)], axis=1
    )
    from_ends = np.concatenate(
        [
            blocks(jm.T, ends, 128, 128).T,
            blocks(dj.T, ends, 128, 128).T,
            blocks(dm.T, ends, 128, 128).T,
        ],
        axis=0,
    )
    to_middle = blocks(jm.T, middle, 256, 256)
    from_middle = np.concatenate([to_middle.T, blocks(dj.T, middle, 256, 256).T], axis=0)

    flow_ends, flow_middle = np.zeros((128, 128)), np.zeros((128, 512))
    sigma_z = np.zeros((1, 512))
    for node, gauss in ends:
        element = 0 if node % 16 == 8 else 120
        flow_ends[element : element + 8, gauss : gauss + 12] = jm.T
        sigma_z[0, gauss : gauss + 12] = sigma
    for t in range(2):
        for node, gauss in middle:
            element = node if node < 128 else node - 128 + 56 * t
            flow_middle[element : element + 8, 256 * t + gauss : 256 * t + gauss + 12] = jm.T
    tile = np.zeros(256)
    for node, gauss in middle:
        tile[gauss : gauss + 12] = sigma
    sigma_z[0, 128:256], sigma_z[0, 256:384], sigma_z[0, 384:] = tile[:128], tile[128:], tile[128:]
    flow_middle = np.concatenate([flow_middle[:, :256], flow_middle[:, 384:]], axis=1)
    sigma_z = np.broadcast_to(sigma_z, (8, 512)).astype(np.float32)
    sigma_xy = np.broadcast_to(np.kron(sigma, sigma)[:, None], (144, 128)).astype(np.float32)

    node_weights = (np.kron(rho, rho)[:, None] * np.tile(rho, 16)[None, :]).astype(np.float32)
    choose_ends = np.zeros((128, 128))
    for node, _ in ends:
        element = 0 if node % 16 == 8 else 120
        choose_ends[element : element + 8, node : node + 8] = np.eye(8)
    return {
        "z_grad": right_table(np.kron(eye16, dm.T)),
        "z_grad_back": right_table(np.kron(eye16, dm)),
        "xy_grad": left_table(np.concatenate([np.kron(dm, eye8), np.kron(eye8, dm)], axis=0)),
        "xy_grad_back": left_table(
            np.concatenate([np.kron(dm.T, eye8), np.kron(eye8, dm.T)], axis=1)
        ),
        "xy_interp": left_table(np.kron(jm, jm)),
        "xy_back_12": left_table(
            np.concatenate([np.kron(dj.T, jm.T), np.kron(jm.T, dj.T)], axis=1)
        ),
        "xy_back_3": left_table(np.kron(jm.T, jm.T)),
        "to_ends": right_table(to_ends),
        "from_ends": right_table(from_ends),
        "to_middle": right_table(to_middle),
        "from_middle": right_table(from_middle),
        "flow_ends": right_table(flow_ends),
        "flow_middle": right_table(flow_middle),
        "choose_ends": choose_ends.astype(ml_dtypes.bfloat16),
        "sigma_xy": sigma_xy,
        "sigma_z": sigma_z,
        "node_weights": node_weights,
    }


def split(value):
    high = value.astype(BF16)
    low = (value - high.astype(F32)).astype(BF16)
    return high, low


def mm(a, b):
    return jnp.dot(a, b, preferred_element_type=F32)


def mm_right(stacked, table):
    return mm(stacked, jnp.concatenate([table[0], table[0], table[1]], axis=0))


def stack_rows(value):
    high, low = split(value)
    return jnp.concatenate([high, low, high], axis=0)


def stack_lanes(value):
    high, low = split(value)
    return jnp.concatenate([high, low, high], axis=1)


def kernel(n_span, n_col, names, *refs):
    n_tables = len(names)
    (adj_h, base_h, md_h, mc_h, jac_h) = refs[:5]
    tables_h = dict(zip(names, refs[5 : 5 + n_tables]))
    out = refs[5 + n_tables]
    refs = refs[6 + n_tables :]
    (v_s, b_s, j_s, md_s, mc_s) = refs[:5]
    tables = dict(zip(names, refs[5 : 5 + n_tables]))
    refs = refs[5 + n_tables :]
    (ue_s, um_s, ge_s, gw_s, xs0, xr0, xs1, xr1, zs, zr, cr) = refs[:11]
    (load_sem, send_sem, recv_sem) = refs[11:]

    span = lax.axis_index("span")
    col = lax.axis_index("col")
    right, left = lax.rem(span + 1, n_span), lax.rem(span + n_span - 1, n_span)
    up, down = lax.rem(col + 1, n_col), lax.rem(col + n_col - 1, n_col)
    x_peers = ((right, col), (left, col))
    has_up, has_down = col < n_col - 1, col > 0

    table = {name: (tables_h[name], tables[name]) for name in names}
    groups = [
        [(base_h, b_s)]
        + [table[n] for n in ("xy_interp", "flow_ends", "sigma_xy", "sigma_z")]
        + [(md_h, md_s), (mc_h, mc_s)]
        + [(adj_h, v_s)]
        + [table[n] for n in ("choose_ends", "node_weights", "to_ends", "xy_grad")],
        [table[n] for n in ("xy_grad_back", "xy_back_12", "xy_back_3", "from_ends")]
        + [(jac_h, j_s)],
        [table[n] for n in ("z_grad", "z_grad_back", "flow_middle", "to_middle", "from_middle")],
    ]
    loads, used = [], 0
    for group in groups:
        loads.append(
            [
                pltpu.make_async_copy(source, target, load_sem.at[used + i])
                for i, (source, target) in enumerate(group)
            ]
        )
        used += len(group)
    for group in loads:
        for copy in group:
            copy.start()

    def arrive(group):
        for copy in loads[group]:
            copy.wait()

    barrier = pltpu.get_barrier_semaphore()

    def greet(peers):
        for peer in peers:
            pl.semaphore_signal(barrier, inc=1, device_id=peer, device_id_type=MESH)

    greet(x_peers)
    pl.when(has_up)(lambda: greet(((span, up), (right, up))))
    pl.when(has_down)(lambda: greet(((span, down), (left, down))))

    def await_peers():
        inside = has_up & has_down
        pl.when(inside)(lambda: pl.semaphore_wait(barrier, 6))
        pl.when(jnp.logical_not(inside))(lambda: pl.semaphore_wait(barrier, 4))

    lanes = [slice(128 * c, 128 * c + 128) for c in range(4)]
    halves_of = [slice(0, 64), slice(64, 128)]
    lane = lax.broadcasted_iota(jnp.int32, (128, 128), 1)
    at_end = (lane < 8) | (lane >= 120)

    def on_left(name, value):
        return mm(tables[name][...], stack_rows(value))

    def pair(i, j):
        return i if i == j else 2 + i + j

    def flux_of(factor, grads):
        return [
            factor(pair(d, 0)) * grads[0]
            + factor(pair(d, 1)) * grads[1]
            + factor(pair(d, 2)) * grads[2]
            for d in range(3)
        ]

    def end_operator(field):
        packed = jnp.where(
            lane < 16,
            pltpu.roll(field[0], 8, 1),
            jnp.where(lane < 32, pltpu.roll(field[1], 24, 1), pltpu.roll(field[2], 40, 1)),
        )
        lines = mm_right(stack_lanes(packed), tables["to_ends"])
        joined = []
        planar = []
        for e in range(2):
            rows = halves_of[e]
            fine = on_left("xy_interp", lines[rows, 128:])
            grads = on_left("xy_grad", packed[rows])
            flux = flux_of(
                lambda slot: ge_s[slot, e], (grads[:64], grads[64:], lines[rows, :128])
            )
            first = jnp.concatenate([ue_s[d, e] * fine for d in range(2)], axis=0)
            back_12 = on_left("xy_back_12", first)
            back_3 = on_left("xy_back_3", ue_s[2, e] * fine)
            planar.append(on_left("xy_grad_back", jnp.concatenate(flux[:2], axis=0)))
            joined.append(jnp.concatenate([back_12, back_3, flux[2]], axis=1))
        normal = mm_right(stack_lanes(jnp.concatenate(joined, axis=0)), tables["from_ends"])
        return normal + jnp.concatenate(planar, axis=0)

    def stiffness(high, low):
        stacked = jnp.concatenate(
            [jnp.concatenate([high[c], low[c], high[c]], axis=1) for c in range(3)], axis=0
        )
        grad_z = mm_right(stacked, tables["z_grad"])
        planar, fluxes = [], [[None, None] for _ in range(3)]
        for e in range(2):
            wide_high = jnp.concatenate([high[c][halves_of[e]] for c in range(3)], axis=1)
            wide_low = jnp.concatenate([low[c][halves_of[e]] for c in range(3)], axis=1)
            grads = mm(
                tables["xy_grad"][...],
                jnp.concatenate([wide_high, wide_low, wide_high], axis=0),
            )
            flux = [[None] * 3 for _ in range(2)]
            for c in range(3):
                start = 128 * c + 64 * e
                g = (grads[:64, lanes[c]], grads[64:, lanes[c]], grad_z[start : start + 64])
                flux[0][c], flux[1][c], fluxes[c][e] = flux_of(lambda slot: gw_s[slot, e], g)
            joined = jnp.concatenate([jnp.concatenate(f, axis=1) for f in flux], axis=0)
            planar.append(on_left("xy_grad_back", joined))
        normal = mm_right(
            stack_lanes(jnp.concatenate([f for two in fluxes for f in two], axis=0)),
            tables["z_grad_back"],
        )
        return jnp.concatenate(planar, axis=0) + jnp.concatenate(
            [normal[128 * c : 128 * c + 128] for c in range(3)], axis=1
        )

    def middle_convection(field, high, low):
        shifted_high, shifted_low = split(pltpu.roll(field[2], 72, 1))
        stacked = jnp.concatenate(
            [
                jnp.concatenate([high[0], high[2], low[0], low[2], high[0], high[2]], axis=1),
                jnp.concatenate(
                    [high[1], shifted_high, low[1], shifted_low, high[1], shifted_high], axis=1
                ),
            ],
            axis=0,
        )
        both = mm_right(stacked, tables["to_middle"])
        lines = jnp.concatenate([both[:128], both[128:]], axis=1)
        pieces = []
        for e in range(2):
            fine = on_left("xy_interp", lines[halves_of[e]])

            def product(d):
                return jnp.concatenate(
                    [
                        um_s[d, e, :, lanes[k]] * fine[:, lanes[i]]
                        for i, k in enumerate((0, 1, 0, 2))
                    ],
                    axis=1,
                )

            first = jnp.concatenate([product(0), product(1)], axis=0)
            pieces.append((on_left("xy_back_12", first), on_left("xy_back_3", product(2))))
        joined = [
            jnp.concatenate([part[:, 256 * t : 256 * t + 256] for part in pieces[e]], axis=1)
            for t in range(2)
            for e in range(2)
        ]
        back = mm_right(stack_lanes(jnp.concatenate(joined, axis=0)), tables["from_middle"])
        tail = back[:128, 128:] + pltpu.roll(back[128:, 128:], 56, 1)
        return jnp.concatenate([back[:128, :128], back[128:, :128], tail], axis=1)

    def with_ends(value, end_tile):
        return jnp.concatenate(
            [
                jnp.where(at_end, pltpu.roll(end_tile, 120 - 16 * c, 1), value[:, lanes[c]])
                for c in range(3)
            ],
            axis=1,
        )

    def local_sum(value, low, high):
        width, count = value.shape[1], high - low
        two = [value[64 * e + 8 * low : 64 * e + 8 * high] for e in range(2)]
        two = [member.reshape(count, 8, width) for member in two]
        place = lax.broadcasted_iota(jnp.int32, (count, 8, width), 1)
        lane = lax.broadcasted_iota(jnp.int32, (8 * count, 128), 1)
        begins = (lane % 8 == 0) & (lane > 0)
        closes = (lane % 8 == 7) & (lane < 127)
        results = []
        for own, other in ((two[0], two[1]), (two[1], two[0])):
            before = pltpu.roll(other, 1, 1)
            after = pltpu.roll(other, 7, 1)
            total = own + jnp.where(place == 7, after, jnp.where(place == 0, before, 0.0))
            total = total.reshape(8 * count, width)
            pieces = []
            for c in range(width // 128):
                piece = total[:, lanes[c]]
                near = jnp.where(
                    closes,
                    pltpu.roll(piece, 127, 1),
                    jnp.where(begins, pltpu.roll(piece, 1, 1), 0.0),
                )
                pieces.append(piece + near)
            results.append(jnp.concatenate(pieces, axis=1))
        return results

    def picks_of(width, find):
        row = lax.broadcasted_iota(jnp.int32, (8, width), 0)
        lane = lax.broadcasted_iota(jnp.int32, (8, width), 1)
        return find(row, lane).astype(F32).astype(BF16)

    picks_out = picks_of(
        256,
        lambda row, lane: ((row < 3) & (lane == 16 * row + 8))
        | ((row >= 4) & (row < 7) & (lane == 16 * (row - 4) + 7))
        | ((row == 3) & (lane == 128))
        | ((row == 7) & (lane == 255)),
    )
    side = lax.broadcasted_iota(jnp.int32, (8, 128), 0)
    place = lax.broadcasted_iota(jnp.int32, (8, 128), 1) % 64

    def remote(source, target, phase, i, peer):
        return pltpu.make_async_remote_copy(
            src_ref=source,
            dst_ref=target,
            send_sem=send_sem.at[phase, i],
            recv_sem=recv_sem.at[phase, i],
            device_id=peer,
            device_id_type=MESH,
        )

    def send_ends(phase, value):
        high, low = split(value)
        picks = picks_out[:, : value.shape[1]]
        contract = (((1,), (1,)), ((), ()))
        tile = lax.dot_general(
            picks, high, contract, preferred_element_type=F32
        ) + lax.dot_general(picks, low, contract, preferred_element_type=F32)
        after = jnp.where(place % 8 == 7, pltpu.roll(tile, 71, 1), 0.0)
        before = jnp.where(place % 8 == 0, pltpu.roll(tile, 57, 1), 0.0)
        zs[phase] = tile + after + before
        tile = zs.at[phase]
        copies = [
            (remote(tile, zr.at[phase, 0], phase, 2, (span, up)), has_up, has_down),
            (remote(tile, zr.at[phase, 1], phase, 3, (span, down)), has_down, has_up),
            (remote(tile, cr.at[phase, 0], phase, 4, (right, up)), has_up, has_down),
            (remote(tile, cr.at[phase, 3], phase, 7, (left, down)), has_down, has_up),
        ]
        if phase == 1:
            copies += [
                (remote(tile, cr.at[phase, 1], phase, 5, (right, down)), has_down, has_up),
                (remote(tile, cr.at[phase, 2], phase, 6, (left, up)), has_up, has_down),
            ]
        for copy, sends, _ in copies:
            pl.when(sends)(copy.start)
        return copies

    sent = []

    def exchange(phase, value, xs, xr, copies):
        faces = [local_sum(value, 7, 8), local_sum(value, 0, 1)]
        for i in range(2):
            for e in range(2):
                xs[i, 8 * e : 8 * e + 8] = faces[i][e]
        x_copies = [
            remote(xs.at[i], xr.at[i], phase, i, peer) for i, peer in enumerate(x_peers)
        ]
        for copy in x_copies:
            copy.start()
        inner = local_sum(value, 1, 7)
        if phase == 0:
            relays = [
                (remote(zr.at[0, 1], cr.at[0, 1], 0, 5, (right, col)), has_up, has_up),
                (remote(zr.at[0, 0], cr.at[0, 2], 0, 6, (left, col)), has_down, has_down),
            ]
            def forward(order):
                for k in order:
                    pl.when(copies[1 - k][2])(copies[1 - k][0].wait_recv)
                    pl.when(relays[k][1])(relays[k][0].start)

            pl.when(col % 2 == 0)(lambda: forward((0, 1)))
            pl.when(col % 2 == 1)(lambda: forward((1, 0)))
            pending = copies[2:] + relays
            all_copies = copies + relays
        else:
            pending = all_copies = copies
        for copy, _, receives in pending:
            pl.when(receives)(copy.wait_recv)
        for copy in x_copies:
            copy.wait_recv()
        from_down = (side >= 4) & has_down
        from_up = (side < 4) & has_up

        def choose(below, above):
            return jnp.where(from_down, below, jnp.where(from_up, above, 0.0))

        lines = choose(zr[phase, 0], zr[phase, 1])
        beside = (choose(cr[phase, 0], cr[phase, 1]), choose(cr[phase, 2], cr[phase, 3]))
        lines = lines + jnp.where(place < 8, pltpu.roll(beside[0], 72, 1), 0.0)
        lines = lines + jnp.where(place >= 56, pltpu.roll(beside[1], 56, 1), 0.0)
        lines = pltpu.roll(lines, 4, 0)
        columns = jnp.transpose(lines)
        added = jnp.concatenate(
            [
                jnp.where(
                    lane == 0,
                    columns[:, c : c + 1],
                    jnp.where(lane == 127, columns[:, 4 + c : 5 + c], 0.0),
                )
                for c in range(value.shape[1] // 128)
            ],
            axis=1,
        )
        pieces = []
        for e in range(2):
            pieces.append(faces[1][e] + xr[0, 8 * e : 8 * e + 8])
            pieces.append(inner[e])
            pieces.append(faces[0][e] + xr[1, 8 * e : 8 * e + 8])
        total = jnp.concatenate(pieces, axis=0) + added
        sent.extend([(copy, True) for copy in x_copies] + [c[:2] for c in all_copies])
        return total

    lane_row = lax.broadcasted_iota(jnp.int32, (1, 128), 1)
    wall = ((lane_row == 0) & (col == 0)) | ((lane_row == 127) & (col == n_col - 1))
    interior = jnp.where(wall, 0.0, 1.0).astype(F32)

    arrive(0)
    fine_rows = []
    for e in range(2):
        rows = jnp.concatenate([b_s[d, :, 8 * e : 8 * e + 8, :].reshape(64, 128) for d in range(3)], axis=1)
        fine = on_left("xy_interp", rows)
        fine_rows.extend(fine[:, lanes[d]] for d in range(3))
    fine_rows = stack_lanes(jnp.concatenate(fine_rows, axis=0))
    fine_weights = tables["sigma_xy"][:, :1] * tables["sigma_z"][:1]
    flow = mm_right(fine_rows, tables["flow_ends"])
    for e in range(2):
        for d in range(3):
            first = 144 * (3 * e + d)
            ue_s[d, e] = flow[first : first + 144] * fine_weights[:, lanes[0]]

    weights = VISCOSITY * tables["node_weights"][...]
    end_weights = jnp.where(
        lane[:64] < 16,
        pltpu.roll(weights, 8, 1),
        jnp.where(lane[:64] < 32, pltpu.roll(weights, 24, 1), pltpu.roll(weights, 40, 1)),
    )
    factors = []
    for name in (md_s, mc_s):
        for i in range(3):
            plane = name[i].astype(F32)
            for e in range(2):
                factors.append(plane[:, 8 * e : 8 * e + 8, :].reshape(64, 128))
    end_factors = mm(
        jnp.concatenate(factors, axis=0).astype(BF16), tables["choose_ends"][...]
    )
    for i, factor in enumerate(factors):
        ge_s[i // 2, i % 2] = end_factors[64 * i : 64 * i + 64] * end_weights
        gw_s[i // 2, i % 2] = factor * weights

    def field_of(c):
        return jnp.concatenate(
            [v_s[c, :, 8 * e : 8 * e + 8, :].reshape(64, 128) for e in range(2)], axis=0
        )

    start = [field_of(c) for c in range(3)]
    arrive(1)
    mass = jnp.concatenate(
        [j_s[:, 8 * e : 8 * e + 8, :].reshape(64, 128) * tables["node_weights"][...] for e in range(2)], axis=0
    )

    arrive(2)
    flow = mm_right(fine_rows, tables["flow_middle"])
    for e in range(2):
        for d in range(3):
            first = 144 * (3 * e + d)
            um_s[d, e] = flow[first : first + 144] * fine_weights[:, 128:]

    pairs = [split(member) for member in start]
    high, low = [p[0] for p in pairs], [p[1] for p in pairs]
    value = middle_convection(start, high, low)
    end_tile = end_operator(start)
    value = value + stiffness(high, low)
    await_peers()
    copies = send_ends(0, jnp.concatenate([end_tile, mass], axis=1))
    value = jnp.concatenate([with_ends(value, end_tile), mass], axis=1)
    total = exchange(0, value, xs0, xr0, copies)
    inverse = 1.0 / total[:, lanes[3]]
    half = [
        interior * (start[c] - (0.5 * STEP_SIZE) * inverse * total[:, lanes[c]]) for c in range(3)
    ]

    end_tile = end_operator(half)
    copies = send_ends(1, end_tile)
    pairs = [split(member) for member in half]
    high, low = [p[0] for p in pairs], [p[1] for p in pairs]
    value = middle_convection(half, high, low) + stiffness(high, low)
    value = with_ends(value, end_tile)
    total = exchange(1, value, xs1, xr1, copies)
    for c in range(3):
        result = interior * (
            field_of(c) - STEP_SIZE * inverse * total[:, lanes[c]]
        )
        for e in range(2):
            out[c, :, 8 * e : 8 * e + 8, :] = result[halves_of[e]].reshape(8, 8, 128)
    for copy, sends in sent:
        if sends is True:
            copy.wait_send()
        else:
            pl.when(sends)(copy.wait_send)


def local(n_span, n_col, adjoint_field, base_flow, metric_diag, metric_cross, jacobian):
    tables = operator_tables()
    table_scratch = [
        pltpu.VMEM(member.shape, jnp.dtype(member.dtype)) for member in tables.values()
    ]
    return pl.pallas_call(
        functools.partial(kernel, n_span, n_col, tuple(tables)),
        out_shape=pltpu.VMEM(adjoint_field.shape, F32),
        in_specs=[pl.BlockSpec(memory_space=pl.ANY)] * (5 + len(tables)),
        out_specs=pl.BlockSpec(memory_space=pltpu.VMEM),
        scratch_shapes=[
            pltpu.VMEM((3, 8, 16, 128), F32),
            pltpu.VMEM((3, 8, 16, 128), F32),
            pltpu.VMEM((8, 16, 128), F32),
            pltpu.VMEM((3, 8, 16, 128), BF16),
            pltpu.VMEM((3, 8, 16, 128), BF16),
            *table_scratch,
            pltpu.VMEM((3, 2, 144, 128), F32),
            pltpu.VMEM((3, 2, 144, 384), F32),
            pltpu.VMEM((6, 2, 64, 128), F32),
            pltpu.VMEM((6, 2, 64, 128), F32),
            pltpu.VMEM((2, 16, 512), F32),
            pltpu.VMEM((2, 16, 512), F32),
            pltpu.VMEM((2, 16, 384), F32),
            pltpu.VMEM((2, 16, 384), F32),
            pltpu.VMEM((2, 8, 128), F32),
            pltpu.VMEM((2, 2, 8, 128), F32),
            pltpu.VMEM((2, 4, 8, 128), F32),
            pltpu.SemaphoreType.DMA((5 + len(tables),)),
            pltpu.SemaphoreType.DMA((2, 8)),
            pltpu.SemaphoreType.DMA((2, 8)),
        ],
        compiler_params=pltpu.CompilerParams(collective_id=0, has_side_effects=True),
    )(
        adjoint_field,
        base_flow,
        metric_diag,
        metric_cross,
        jacobian,
        *[jnp.asarray(member) for member in tables.values()],
    )


def solution(mesh):
    in_specs = (
        P(None, "span", None, "col"),
        P(None, "span", None, "col"),
        P(None, "span", None, "col"),
        P(None, "span", None, "col"),
        P("span", None, "col"),
    )
    out_specs = P(None, "span", None, "col")
    body = functools.partial(local, mesh.shape["span"], mesh.shape["col"])
    return jax.shard_map(body, mesh=mesh, in_specs=in_specs, out_specs=out_specs, check_vma=False)
```
